128 devices in a mesh: tm: 16 (over z, y_hi, core), head: 8 (over y_lo, x).
Axes of the slice: x: 4, y: 4 (y_hi: 2, y_lo: 2; y = y_hi * 2 + y_lo), z: 4, core: 2. Of those that a mesh axis runs over, the one named last changes fastest.
Arguments:
- query: bfloat16 [20480, 24, 128], P(('tm', 'head')), may hold values from -15 to 15
- key: bfloat16 [20480, 24, 128], P(('tm', 'head')), may hold values from -15 to 15
- value: bfloat16 [20480, 24, 128], P(('tm', 'head')), may hold values from -6 to 6
- far_list: int32 [160, 16], P('tm'), may hold values from 0 to 159, as said below
- far_count: int32 [160, 16], P('tm'), may hold values from 0 to 1, as said below
Outputs:
- attended: bfloat16 [20480, 24, 128], P(('tm', 'head'))
The draws below stay inside these ranges and needn't reach their ends.
Inputs may be any that keep to these rules, and one draw needn't show every extreme that they name: far_list[b, g] is a block of frame g: far_list[b, g] // 10 == g. far_count[b, g] is 0 where the frame of block b and frame g are less than 2 apart. For frames f and g at distance d >= 2, exactly min(5, max(1, 2, 2 * 5 // d)) of the 10 blocks of frame f have far_count 1 for g; so at most 5 blocks of a frame list blocks of one other frame, and exactly 5 at distance 2.
All inputs are finite; a program needn't handle non-finite values.
Results may differ from the reference program's by a relative error of at most 0.012.
Values may be sent and summed in bfloat16 or wider, within the bound.
No kernel may reach another device: no remote copies, remote signals or barrier semaphores. Data moves between devices by JAX's collectives and lax.ppermute only.
A program may use at most 128 MiB of HBM per device.

```python
import jax
import jax.numpy as jnp
from jax import lax

FW = 80
BLK = 128
DH = 128
RT = 16
RH = 56
RW = 56
HEADS = 24
FRAME_TOK = 1280
FRAMES = 16
TOKENS = 20480
BLOCKS = 160
FRAME_BLOCKS = 10
CAP = 5


def loose_rows(key, spread, salt):
    fresh = jax.random.fold_in(key, salt)
    return jnp.clip(jax.random.normal(fresh, (TOKENS, HEADS, DH), jnp.float32) * spread, -15.0, 15.0)


def draw_query(key, part):
    drawn = loose_rows(key, 2.5, 1)
    return drawn.astype(jnp.bfloat16)


def draw_key(key, part):
    drawn = loose_rows(key, 1.0, 2)
    return drawn.astype(jnp.bfloat16)


def one_permutation(pair_key):
    return jax.random.permutation(pair_key, FRAME_BLOCKS)


def mask_tables(key):
    salt = jax.random.fold_in(key, 777)
    block_frame = jnp.arange(BLOCKS) // FRAME_BLOCKS
    source = jnp.arange(FRAMES)
    frame_gap = jnp.abs(block_frame[:, None] - source[None, :])
    quota = jnp.minimum(CAP, jnp.maximum(jnp.maximum(1, 2 * CAP // 5), 2 * CAP // jnp.maximum(frame_gap, 1)))
    pair_keys = jax.random.split(jax.random.fold_in(salt, 1), FRAMES * FRAMES)
    ranks = jax.vmap(one_permutation)(pair_keys)
    ranks = ranks.reshape(FRAMES, FRAMES, FRAME_BLOCKS).transpose(0, 2, 1).reshape(BLOCKS, FRAMES)
    listed = ((frame_gap >= 2) & (ranks < quota)).astype(jnp.int32)
    local_ids = jax.random.randint(jax.random.fold_in(salt, 2), (BLOCKS, FRAMES), 0, FRAME_BLOCKS)
    return ((source[None, :] * FRAME_BLOCKS + local_ids).astype(jnp.int32), listed)


def draw_far_list(key, part):
    return mask_tables(key)[0]


def draw_far_count(key, part):
    return mask_tables(key)[1]


def block_levels(own_key, shape, shards, smallest, high):
    level, own = 1.0, jax.random.fold_in(own_key, 6)
    for position, shards_of in shards:
        steps = jnp.exp(jax.random.uniform(jax.random.fold_in(own, position), (shards_of,), jnp.float32, smallest / len(shards), high / len(shards)))
        level = level * jnp.repeat(steps, shape[position] // shards_of).reshape([-1 if axis == position else 1 for axis in range(len(shape))])
    return level


def bell_draw(own_key, extent, scale, bound, cuts=(), kind=jnp.bfloat16):
    entries = jax.random.normal(own_key, extent, jnp.float32) * scale
    if len(cuts) > 0:
        entries = block_levels(own_key, extent, cuts, -0.22, 0.18) * entries
    return jnp.clip(entries, min=-bound, max=bound).astype(kind)


def setup_inputs(seed: int = 0) -> dict:
    arg_keys = jax.random.split(jax.random.key(seed), 6)
    query = draw_query(jax.random.fold_in(arg_keys[5], 71), 0)
    key = draw_key(jax.random.fold_in(arg_keys[5], 71), 0)
    value = bell_draw(arg_keys[2], (TOKENS, HEADS, DH), 1.0, 6.0, ((0, 128),))
    far_list = draw_far_list(jax.random.fold_in(arg_keys[5], 71), 0)
    far_count = draw_far_count(jax.random.fold_in(arg_keys[5], 71), 0)
    return dict(query=query, key=key, value=value, far_list=far_list, far_count=far_count)


THETA = 256.0


def swap_matrix(head_width):
    row_ids = jnp.arange(head_width)[:, None]
    col_ids = jnp.arange(head_width)[None, :]
    minus_one = (row_ids == col_ids + 1) & (col_ids % 2 == 0)
    plus_one = (col_ids == row_ids + 1) & (row_ids % 2 == 0)
    return jnp.where(plus_one, 1.0, jnp.where(minus_one, -1.0, 0.0)).astype(jnp.bfloat16)


def axis_angles(positions, span_width):
    pair_index = jnp.arange(span_width // 2).astype(jnp.float32)
    inverse = THETA ** (-2.0 * pair_index / span_width)
    return positions[:, None] * inverse[None, :]


def rotate(values, frame_pos, row_pos, col_pos):
    token_count, head_count, head_width = values.shape
    angles = jnp.concatenate([axis_angles(frame_pos, RT), axis_angles(row_pos, RH), axis_angles(col_pos, RW)], axis=1)
    angles = jnp.repeat(angles, 2, axis=1)
    swapped = jnp.dot(values.reshape(token_count * head_count, head_width), swap_matrix(head_width), preferred_element_type=jnp.float32)
    swapped = swapped.reshape(token_count, head_count, head_width)
    turned = values.astype(jnp.float32) * jnp.cos(angles)[:, None, :] + swapped * jnp.sin(angles)[:, None, :]
    return turned.astype(jnp.bfloat16)


def reference(query, key, value, far_list, far_count):
    token_index = jnp.arange(TOKENS, dtype=jnp.int32)
    frame_pos = (token_index // FRAME_TOK).astype(jnp.float32)
    row_pos = ((token_index % FRAME_TOK) // FW).astype(jnp.float32)
    col_pos = (token_index % FW).astype(jnp.float32)
    turned_q = lax.optimization_barrier(jnp.transpose(rotate(query, frame_pos, row_pos, col_pos), (1, 0, 2)))
    turned_k = lax.optimization_barrier(jnp.transpose(rotate(key, frame_pos, row_pos, col_pos), (1, 0, 2)))
    values_t = jnp.transpose(value, (1, 0, 2))
    score_scale = DH ** -0.5
    padded_k = jnp.pad(turned_k, ((0, 0), (FRAME_TOK, FRAME_TOK), (0, 0)))
    padded_v = jnp.pad(values_t, ((0, 0), (FRAME_TOK, FRAME_TOK), (0, 0)))
    key_blocks = turned_k.reshape(HEADS, BLOCKS, BLK, DH)
    value_blocks = values_t.reshape(HEADS, BLOCKS, BLK, DH)

    def one_block(block):
        frame_index = (block // FRAME_BLOCKS).astype(jnp.int32)
        query_rows = lax.dynamic_slice_in_dim(turned_q, (block * BLK).astype(jnp.int32), BLK, 1)
        near_keys = lax.dynamic_slice_in_dim(padded_k, (frame_index * FRAME_TOK).astype(jnp.int32), 3 * FRAME_TOK, 1)
        near_values = lax.dynamic_slice_in_dim(padded_v, (frame_index * FRAME_TOK).astype(jnp.int32), 3 * FRAME_TOK, 1)
        key_frame = jnp.arange(3 * FRAME_TOK, dtype=jnp.int32) // FRAME_TOK + frame_index - 1
        near_ok = (key_frame >= 0) & (key_frame < FRAMES)
        far_ids = far_list[block].astype(jnp.int32)
        far_keys = jnp.take(key_blocks, far_ids, axis=1).reshape(HEADS, FRAMES * BLK, DH)
        far_values = jnp.take(value_blocks, far_ids, axis=1).reshape(HEADS, FRAMES * BLK, DH)
        far_ok = jnp.repeat(far_count[block] > 0, BLK)
        keys_all = jnp.concatenate([near_keys, far_keys], axis=1)
        values_all = jnp.concatenate([near_values, far_values], axis=1)
        valid = jnp.concatenate([near_ok, far_ok], axis=0)
        scores = jnp.einsum("hid,hjd->hij", query_rows.astype(jnp.float32), keys_all.astype(jnp.float32)) * score_scale
        scores = jnp.where(valid[None, None, :], scores, -jnp.inf)
        row_max = jnp.max(scores, axis=2)
        weights = jnp.exp(scores - row_max[..., None])
        row_total = jnp.sum(weights, axis=2)
        rounded = lax.optimization_barrier(weights.astype(jnp.bfloat16))
        mixed = jnp.einsum("hij,hjd->hid", rounded.astype(jnp.float32), values_all.astype(jnp.float32))
        return (mixed / row_total[..., None]).astype(jnp.bfloat16)

    attended = lax.map(one_block, jnp.arange(BLOCKS, dtype=jnp.int32))
    return jnp.transpose(attended, (0, 2, 1, 3)).reshape(TOKENS, HEADS, DH)
```

```python
import jax
import jax.numpy as jnp
import numpy as np
from jax import lax
from jax.experimental import pallas as pl
from jax.experimental.pallas import tpu as pltpu
from jax.sharding import Mesh
from jax.sharding import PartitionSpec as P

FW = 80
TOK = 1280
BLK = 128
CH = 160
NB = 10
DH = 128
RT, RH, RW = 16, 56, 56
HEADS = 24
PER = 3
PLANE = 4
THETA = 256.0
SCALE = float(DH**-0.5 * np.log2(np.e))
CHUNKS = ((0, 1, 2),)

BASE = 8
BIG, MID, ONE = 12, 4, 1
BIG_AT, MID_AT, ONE_AT = 32, 44, 48
VMEM = 58 * 2**20

i32 = jnp.int32


def params():
    return pltpu.CompilerParams(vmem_limit_bytes=VMEM)


def smem():
    return pl.BlockSpec(memory_space=pltpu.SMEM)


def table_body(place_ref, list_ref, count_ref, want_ref, qslot_ref, plane_ref, kb_ref, qb_ref):
    z, r = place_ref[0], place_ref[1]
    f = PLANE * z + r

    def frame_lists(g, carry):
        for j in range(8):
            kb_ref[g * 8 + j] = 0
            qb_ref[g * 8 + j] = 0

        def one_block(n, filled):
            kb_ref[g * 8 + filled] = list_ref[n, g] - NB * g
            qb_ref[g * 8 + filled] = n
            return filled + jnp.where(count_ref[n, g] > 0, 1, 0).astype(i32)

        lax.fori_loop(0, NB, one_block, jnp.int32(0))
        return carry

    lax.fori_loop(0, PLANE * 4, frame_lists, jnp.int32(0))

    def clear(s, carry):
        for zp in range(4):
            want_ref[zp, s] = 0
        return carry

    lax.fori_loop(0, 128, clear, jnp.int32(0))
    for s in range(64):
        qslot_ref[s] = -1
    for zp in range(4):
        for i in range(PLANE):
            g = PLANE * zp + i
            far = jnp.abs(f - g) >= 2
            for j in range(2):
                want_ref[zp, 2 * i + j] = NB * i + kb_ref[g * 8 + j]
                qslot_ref[zp * BASE + 2 * i + j] = jnp.where(far & (z != zp), qb_ref[g * 8 + j], -1)

    def listed(zp, s, slot, i, j):
        at = (PLANE * zp + i) * 8 + j
        want_ref[zp, s] = NB * i + kb_ref[at]
        qslot_ref[slot] = qb_ref[at]

    def side(up, first, second, third):
        zp = z - 1 if up else z + 1
        exists = z > 0 if up else z < 3
        near, two, three = (3, 2, 1) if up else (0, 1, 2)

        @pl.when(exists & (r == first))
        def _():
            for j in range(2):
                listed(zp, 2 * near + j, zp * BASE + 2 * near + j, two, 2 + j)
            for n in range(NB):
                want_ref[zp, BASE + n] = NB * near + n
            listed(zp, BASE + 10, BIG_AT + 10, two, 4)
            listed(zp, BASE + 11, BIG_AT + 11, three, 2)

        @pl.when(exists & (r == second))
        def _():
            for j in range(3):
                listed(zp, BASE + BIG + j, MID_AT + j, near, 2 + j)
            listed(zp, BASE + BIG + 3, MID_AT + 3, two, 2)

        @pl.when(exists & (r == third))
        def _():
            listed(zp, BASE + BIG + MID, ONE_AT, near, 2)

    side(True, 0, 1, 2)
    side(False, 3, 2, 1)

    two = (r + 2) % PLANE
    three = PLANE - 1 - r
    for j in range(5):
        at = (PLANE * z + two) * 8 + j
        plane_ref[2 * j] = qb_ref[at]
        plane_ref[2 * j + 1] = NB * two + kb_ref[at]
    for j in range(3):
        at = (PLANE * z + three) * 8 + j
        plane_ref[10 + 2 * j] = qb_ref[at]
        plane_ref[10 + 2 * j + 1] = NB * three + kb_ref[at]


def tables(place, far_list, far_count):
    return pl.pallas_call(
        table_body,
        in_specs=[smem(), smem(), smem()],
        out_specs=[smem(), smem(), smem()],
        out_shape=[
            jax.ShapeDtypeStruct((4, 128), i32),
            jax.ShapeDtypeStruct((64,), i32),
            jax.ShapeDtypeStruct((16,), i32),
        ],
        scratch_shapes=[pltpu.SMEM((128,), i32), pltpu.SMEM((128,), i32)],
        name="tables",
    )(place, far_list, far_count)


def lane_rates():
    rates = []
    for width in (RT, RH, RW):
        rates.append(np.float32(THETA) ** (np.float32(-2.0) * np.arange(width // 2, dtype=np.float32) / np.float32(width)))
    return np.repeat(np.concatenate(rates), 2)[None].astype(np.float32)


def turn_tables(frame, chunk, rates):
    lane = lax.broadcasted_iota(i32, (CH, DH), 1)
    token = lax.broadcasted_iota(i32, (CH, DH), 0)
    below = (token >= FW).astype(i32)
    position = jnp.where(lane < RT, frame, jnp.where(lane < RT + RH, 2 * chunk + below, token - FW * below))
    angle = position.astype(jnp.float32) * rates
    even = lane % 2 == 0
    sine = jnp.sin(angle)
    return jnp.cos(angle), jnp.where(even, -sine, sine), even


def turn(x, tables_):
    cosine, sine, even = tables_
    swapped = jnp.where(even, pltpu.roll(x, DH - 1, 1), pltpu.roll(x, 1, 1))
    return x * cosine + swapped * sine


def enter_kv_body(rows, place_ref, rates_ref, k_ref, v_ref, o_ref, ks, vs):
    tabs = turn_tables(place_ref[2], place_ref[3], rates_ref[...])
    ks[...] = k_ref[...].astype(jnp.float32).reshape(CH * HEADS, DH)
    vs[...] = v_ref[...].astype(jnp.float32).reshape(CH * HEADS, DH)
    for hd in range(8):
        for at, row in enumerate(rows):
            pick = pl.ds(hd * PER + row, CH, stride=HEADS)
            turned = turn(ks[pick, :], tabs).astype(jnp.bfloat16)
            kept = vs[pick, :].astype(jnp.bfloat16)
            for yh in range(2):
                o_ref[yh, hd, at, 0] = turned
                o_ref[yh, hd, at, 1] = kept


def enter_kv(place, rates, key, value, rows):
    return pl.pallas_call(
        lambda *refs: enter_kv_body(rows, *refs),
        in_specs=[smem()] + [pl.BlockSpec(memory_space=pltpu.VMEM)] * 3,
        out_specs=pl.BlockSpec(memory_space=pltpu.VMEM),
        out_shape=jax.ShapeDtypeStruct((2, 8, len(rows), 2, CH, DH), jnp.bfloat16),
        scratch_shapes=[pltpu.VMEM((CH * HEADS, DH), jnp.float32)] * 2,
        compiler_params=params(),
        name="enter_kv",
    )(place, rates, key, value)


def enter_q_body(rows, place_ref, rates_ref, q_ref, o_ref, qs):
    tabs = turn_tables(place_ref[2], place_ref[3], rates_ref[...])
    qs[...] = q_ref[...].astype(jnp.float32).reshape(CH * HEADS, DH)
    for hd in range(8):
        for at, row in enumerate(rows):
            pick = pl.ds(hd * PER + row, CH, stride=HEADS)
            o_ref[hd, at] = turn(qs[pick, :], tabs).astype(jnp.bfloat16)


def enter_q(place, rates, query, rows):
    return pl.pallas_call(
        lambda *refs: enter_q_body(rows, *refs),
        in_specs=[smem()] + [pl.BlockSpec(memory_space=pltpu.VMEM)] * 2,
        out_specs=pl.BlockSpec(memory_space=pltpu.VMEM),
        out_shape=jax.ShapeDtypeStruct((8, len(rows), CH, DH), jnp.bfloat16),
        scratch_shapes=[pltpu.VMEM((CH * HEADS, DH), jnp.float32)],
        compiler_params=params(),
        name="enter_q",
    )(place, rates, query)


def pack_body(place_ref, want_ref, own_ref, sib_ref, base_ref, big_ref, mid_ref, one_ref, frames):
    z, r, c = place_ref[0], place_ref[1], place_ref[4]
    for b in range(2):
        for ref, core in ((own_ref, c), (sib_ref, 1 - c)):
            start = pl.multiple_of((2 * b + core) * TOK, TOK)
            frames[pl.ds(start, TOK), :] = ref[b, :, 0, 0].reshape(TOK, DH)

    def block(index):
        return frames[pl.ds(pl.multiple_of(index * BLK, BLK), BLK), :]

    for zp in range(4):
        for s in range(BASE):
            base_ref[zp, s, 0, 0] = block(want_ref[zp, s])
    low, high = jnp.minimum(z + 1, 3), jnp.maximum(z - 1, 0)
    outer = jnp.where(r < 2, low, high)
    inner = jnp.where(r < 2, high, low)
    for s in range(BIG):
        big_ref[s, 0, 0] = block(want_ref[outer, BASE + s])
    for s in range(MID):
        mid_ref[s, 0, 0] = block(want_ref[outer, BASE + BIG + s])
    one_ref[0, 0, 0] = block(want_ref[inner, BASE + BIG + MID])


def pack(place, asked, own, sib):
    nh = own.shape[2]
    whole = pl.BlockSpec((2, 8, 1, 1, CH, DH), lambda h, kv: (0, 0, h, kv, 0, 0))

    def out(*lead):
        zeros = (0,) * len(lead)
        return pl.BlockSpec((*lead, 1, 1, BLK, DH), lambda h, kv: (*zeros, h, kv, 0, 0))

    def shape(*lead):
        return jax.ShapeDtypeStruct((*lead, nh, 2, BLK, DH), jnp.bfloat16)

    return pl.pallas_call(
        pack_body,
        grid=(nh, 2),
        in_specs=[smem(), smem(), whole, whole],
        out_specs=[out(4, BASE), out(BIG), out(MID), out(ONE)],
        out_shape=[shape(4, BASE), shape(BIG), shape(MID), shape(ONE)],
        scratch_shapes=[pltpu.VMEM((PLANE * TOK, DH), jnp.bfloat16)],
        compiler_params=params(),
        name="pack",
    )(place, asked, own, sib)


def dot_t(a, b):
    return lax.dot_general(a, b, (((1,), (1,)), ((), ())), preferred_element_type=jnp.float32)


def flash(q, k, v, rows, m_ref, l_ref, acc_ref, first=False):
    s = dot_t(q, k) * SCALE
    top = jnp.max(s, axis=1, keepdims=True)
    if first:
        m_new = jnp.broadcast_to(top, (q.shape[0], DH))
    else:
        m_old = m_ref[rows, :]
        m_new = jnp.maximum(m_old, top)
    p = jnp.exp2(s - m_new[:, :1])
    total = jnp.sum(p, axis=1, keepdims=True)
    mixed = jnp.dot(p.astype(jnp.bfloat16), v, preferred_element_type=jnp.float32)
    if first:
        l_ref[rows, :] = jnp.broadcast_to(total, (q.shape[0], DH))
        acc_ref[rows, :] = mixed
    else:
        fade = jnp.exp2(m_old - m_new)
        l_ref[rows, :] = l_ref[rows, :] * fade + total
        acc_ref[rows, :] = acc_ref[rows, :] * fade + mixed
    m_ref[rows, :] = m_new


QT = 256


def near_body(place_ref, plane_ref, q_ref, own_ref, sib_ref, acc_ref, m_ref, l_ref, qs, kf, vf):
    r, c = place_ref[1], place_ref[4]
    qs[...] = q_ref[:, 0].reshape(TOK, DH)
    for b in range(2):
        for ref, core in ((own_ref, c), (sib_ref, 1 - c)):
            start = pl.multiple_of((2 * b + core) * TOK, TOK)
            kf[pl.ds(start, TOK), :] = ref[b, :, 0, 0].reshape(TOK, DH)
            vf[pl.ds(start, TOK), :] = ref[b, :, 0, 1].reshape(TOK, DH)
    acc, m, l = acc_ref.at[0], m_ref.at[0], l_ref.at[0]

    def frame(i, first):
        at = pl.ds(pl.multiple_of(i * TOK, TOK), TOK)

        def tile(t, carry):
            rows = pl.ds(pl.multiple_of(t * QT, QT), QT)
            flash(qs[rows, :], kf[at, :], vf[at, :], rows, m, l, acc, first)
            return carry

        lax.fori_loop(0, TOK // QT, tile, jnp.int32(0))

    frame(r, True)

    @pl.when(r > 0)
    def _():
        frame(r - 1, False)

    @pl.when(r < PLANE - 1)
    def _():
        frame(r + 1, False)

    def pair(p, carry):
        rows = pl.ds(pl.multiple_of(plane_ref[2 * p] * BLK, BLK), BLK)
        at = pl.ds(pl.multiple_of(plane_ref[2 * p + 1] * BLK, BLK), BLK)
        flash(qs[rows, :], kf[at, :], vf[at, :], rows, m, l, acc)
        return carry

    lax.fori_loop(0, jnp.where((r == 0) | (r == PLANE - 1), 8, 5), pair, jnp.int32(0))


def near(place, plane_pairs, q, own, sib):
    nh = q.shape[1]
    frames = pl.BlockSpec((2, 8, 1, 2, CH, DH), lambda h: (0, 0, h, 0, 0, 0))
    state = pl.BlockSpec((1, TOK, DH), lambda h: (h, 0, 0))
    return pl.pallas_call(
        near_body,
        grid=(nh,),
        in_specs=[smem(), smem(), pl.BlockSpec((8, 1, CH, DH), lambda h: (0, h, 0, 0)), frames, frames],
        out_specs=[state] * 3,
        out_shape=[jax.ShapeDtypeStruct((nh, TOK, DH), jnp.float32)] * 3,
        scratch_shapes=[
            pltpu.VMEM((TOK, DH), jnp.bfloat16),
            pltpu.VMEM((PLANE * TOK, DH), jnp.bfloat16),
            pltpu.VMEM((PLANE * TOK, DH), jnp.bfloat16),
        ],
        compiler_params=params(),
        cost_estimate=pl.CostEstimate(
            flops=nh * 3 * TOK * TOK * DH * 4, transcendentals=nh * 3 * TOK * TOK, bytes_accessed=nh * 4 * 2**20
        ),
        name="near",
    )(place, plane_pairs, q, own, sib)


def far_body(
    place_ref, qslot_ref, q_ref, acc_in, m_in, l_in, base_ref, big_ref, mid_ref, one_ref, o_ref, qs, acc, m, l
):
    z, r = place_ref[0], place_ref[1]
    qs[...] = q_ref[:, 0].reshape(TOK, DH)
    acc[...] = acc_in[0]
    m[...] = m_in[0]
    l[...] = l_in[0]

    @pl.when(((r == 0) & (z > 0)) | ((r == PLANE - 1) & (z < 3)))
    def _():
        def tile(t, carry):
            rows = pl.ds(pl.multiple_of(t * QT, QT), QT)
            k = big_ref[:NB, 0, 0].reshape(TOK, DH)
            v = big_ref[:NB, 0, 1].reshape(TOK, DH)
            flash(qs[rows, :], k, v, rows, m, l, acc)
            return carry

        lax.fori_loop(0, TOK // QT, tile, jnp.int32(0))

    def pair(slot, k, v):
        block = qslot_ref[slot]

        @pl.when(block >= 0)
        def _():
            rows = pl.ds(pl.multiple_of(block * BLK, BLK), BLK)
            flash(qs[rows, :], k(), v(), rows, m, l, acc)

    def base(s, carry):
        pair(s, lambda: base_ref[s // BASE, s % BASE, 0, 0], lambda: base_ref[s // BASE, s % BASE, 0, 1])
        return carry

    lax.fori_loop(0, 4 * BASE, base, jnp.int32(0))
    for s in (10, 11):
        pair(BIG_AT + s, lambda: big_ref[s, 0, 0], lambda: big_ref[s, 0, 1])
    for s in range(MID):
        pair(MID_AT + s, lambda: mid_ref[s, 0, 0], lambda: mid_ref[s, 0, 1])
    pair(ONE_AT, lambda: one_ref[0, 0, 0], lambda: one_ref[0, 0, 1])
    o_ref[:, 0] = (acc[...] / l[...]).astype(jnp.bfloat16).reshape(8, CH, DH)


def far(place, qslot, q, state, base, big, mid, one):
    nh = q.shape[1]
    tokens = pl.BlockSpec((8, 1, CH, DH), lambda h: (0, h, 0, 0))
    held = pl.BlockSpec((1, TOK, DH), lambda h: (h, 0, 0))

    def blocks(*lead):
        zeros = (0,) * len(lead)
        return pl.BlockSpec((*lead, 1, 2, BLK, DH), lambda h: (*zeros, h, 0, 0, 0))

    return pl.pallas_call(
        far_body,
        grid=(nh,),
        in_specs=[smem(), smem(), tokens, held, held, held, blocks(4, BASE), blocks(BIG), blocks(MID), blocks(ONE)],
        out_specs=tokens,
        out_shape=jax.ShapeDtypeStruct((8, nh, CH, DH), jnp.bfloat16),
        scratch_shapes=[pltpu.VMEM((TOK, DH), jnp.bfloat16)] + [pltpu.VMEM((TOK, DH), jnp.float32)] * 3,
        compiler_params=params(),
        name="far",
    )(place, qslot, q, *state, base, big, mid, one)


def leave_body(groups, *refs):
    *in_refs, o_ref, s = refs
    for ref, rows in zip(in_refs, groups, strict=True):
        for hd in range(8):
            for at, row in enumerate(rows):
                s[pl.ds(hd * PER + row, CH, stride=HEADS), :] = ref[hd, at].astype(jnp.float32)
    o_ref[...] = s[...].reshape(CH, HEADS, DH).astype(jnp.bfloat16)


def leave(parts, groups):
    return pl.pallas_call(
        lambda *refs: leave_body(groups, *refs),
        in_specs=[pl.BlockSpec(memory_space=pltpu.VMEM)] * len(parts),
        out_specs=pl.BlockSpec(memory_space=pltpu.VMEM),
        out_shape=jax.ShapeDtypeStruct((CH, HEADS, DH), jnp.bfloat16),
        scratch_shapes=[pltpu.VMEM((CH * HEADS, DH), jnp.float32)],
        compiler_params=params(),
        name="leave",
    )(*parts)


def at_plane(z, r):
    return PLANE * z + r


TM = ("z", "yh", "c")
BIG_PAIRS = [(at_plane(z, 0), at_plane(z + 1, 0)) for z in range(3)] + [(at_plane(z + 1, 3), at_plane(z, 3)) for z in range(3)]
MID_PAIRS = [(at_plane(z, 1), at_plane(z + 1, 1)) for z in range(3)] + [(at_plane(z + 1, 2), at_plane(z, 2)) for z in range(3)]
ONE_PAIRS = [(at_plane(z, 2), at_plane(z + 1, 2)) for z in range(3)] + [(at_plane(z + 1, 1), at_plane(z, 1)) for z in range(3)]


def shards(query, key, value, far_list, far_count):
    z, yh, c, hd = (lax.axis_index(a) for a in ("z", "yh", "c", "head"))
    r = 2 * yh + c
    place = jnp.stack([z, r, PLANE * z + r, hd, c]).astype(i32)
    rates = jnp.asarray(lane_rates())
    want, qslot, plane_pairs = tables(place, far_list, far_count)
    asked = lax.all_to_all(want, "z", 0, 0, tiled=True)
    parts = []
    for rows in CHUNKS:
        sent = enter_kv(place, rates, key, value, rows)
        own = lax.all_to_all(sent.reshape(16, len(rows), 2, CH, DH), ("yh", "head"), 0, 0, tiled=True)
        own = own.reshape(2, 8, len(rows), 2, CH, DH)
        sib = lax.ppermute(own, "c", [(0, 1), (1, 0)])
        q = lax.all_to_all(enter_q(place, rates, query, rows), "head", 0, 0, tiled=True)
        base, big, mid, one = pack(place, asked, own, sib)
        big = lax.ppermute(big, TM, BIG_PAIRS)
        base = lax.all_to_all(base, "z", 0, 0, tiled=True)
        mid = lax.ppermute(mid, TM, MID_PAIRS)
        one = lax.ppermute(one, TM, ONE_PAIRS)
        state = near(place, plane_pairs, q, own, sib)
        out = far(place, qslot, q, state, base, big, mid, one)
        parts.append(lax.all_to_all(out, "head", 0, 0, tiled=True))
    return leave(parts, CHUNKS)


def solution(mesh):
    split = Mesh(mesh.devices.reshape(4, 2, 2, 8), ("z", "yh", "c", "head"))
    tokens = P(("z", "yh", "c", "head"), None, None)
    blocks = P(TM, None)
    return jax.shard_map(
        shards,
        mesh=split,
        in_specs=(tokens, tokens, tokens, blocks, blocks),
        out_specs=tokens,
        check_vma=False,
    )
```

```python
import jax
import jax.numpy as jnp
import numpy as np
from jax import lax
from jax.experimental import pallas as pl
from jax.experimental.pallas import tpu as pltpu
from jax.sharding import Mesh
from jax.sharding import PartitionSpec as P

FW = 80
TOK = 1280
BLK = 128
CH = 160
NB = 10
DH = 128
RT, RH, RW = 16, 56, 56
HEADS = 24
PER = 3
PLANE = 4
THETA = 256.0
SCALE = float(DH**-0.5 * np.log2(np.e))
CHUNKS = ((0,), (1, 2))

BASE = 8
BESIDE = 9
BIG = 11
MID = 3
VMEM = 58 * 2**20

i32 = jnp.int32


def params():
    return pltpu.CompilerParams(vmem_limit_bytes=VMEM)


def smem():
    return pl.BlockSpec(memory_space=pltpu.SMEM)


def table_body(place_ref, list_ref, count_ref, want_ref, qslot_ref, late_ref, plane_ref, kb_ref, qb_ref):
    z, r = place_ref[0], place_ref[1]
    f = PLANE * z + r

    def frame_lists(g, carry):
        for j in range(8):
            kb_ref[g * 8 + j] = 0
            qb_ref[g * 8 + j] = 0

        def one_block(n, filled):
            kb_ref[g * 8 + filled] = list_ref[n, g] - NB * g
            qb_ref[g * 8 + filled] = n
            return filled + jnp.where(count_ref[n, g] > 0, 1, 0).astype(i32)

        lax.fori_loop(0, NB, one_block, jnp.int32(0))
        return carry

    lax.fori_loop(0, PLANE * 4, frame_lists, jnp.int32(0))

    def clear(s, carry):
        for zp in range(4):
            want_ref[zp, s] = 0
        return carry

    lax.fori_loop(0, 128, clear, jnp.int32(0))
    for s in range(64):
        qslot_ref[s] = -1
    for s in range(MID):
        late_ref[s] = -1
    for zp in range(4):
        for i in range(PLANE):
            g = PLANE * zp + i
            far = jnp.abs(f - g) >= 2
            for j in range(2):
                want_ref[zp, 2 * i + j] = NB * i + kb_ref[g * 8 + j]
                qslot_ref[zp * BESIDE + 2 * i + j] = jnp.where(far & (z != zp), qb_ref[g * 8 + j], -1)

    def listed(zp, s, i, j):
        at = (PLANE * zp + i) * 8 + j
        want_ref[zp, s] = NB * i + kb_ref[at]
        qslot_ref[zp * BESIDE + s] = qb_ref[at]

    def side(up, first, second, third):
        zp = z - 1 if up else z + 1
        exists = z > 0 if up else z < 3
        near, two, three = (3, 2, 1) if up else (0, 1, 2)

        @pl.when(exists & (r == first))
        def _():
            for j in range(2):
                listed(zp, 2 * near + j, two, 2 + j)
            listed(zp, BASE, two, 4)
            for n in range(NB):
                want_ref[zp, BESIDE + n] = NB * near + n
            at = (PLANE * zp + three) * 8 + 2
            want_ref[zp, BESIDE + NB] = NB * three + kb_ref[at]
            late_ref[0] = qb_ref[at]

        @pl.when(exists & (r == second))
        def _():
            listed(zp, BASE, two, 2)
            for j in range(MID):
                at = (PLANE * zp + near) * 8 + 2 + j
                want_ref[zp, BESIDE + BIG + j] = NB * near + kb_ref[at]
                late_ref[j] = qb_ref[at]

        @pl.when(exists & (r == third))
        def _():
            listed(zp, BASE, near, 2)

    side(True, 0, 1, 2)
    side(False, 3, 2, 1)

    two = (r + 2) % PLANE
    three = PLANE - 1 - r
    outer = (r == 0) | (r == PLANE - 1)
    for j in range(5):
        at = (PLANE * z + two) * 8 + j
        plane_ref[2 * j] = qb_ref[at]
        plane_ref[2 * j + 1] = NB * two + kb_ref[at]
    for j in range(3):
        at = (PLANE * z + three) * 8 + j
        plane_ref[10 + 2 * j] = jnp.where(outer, qb_ref[at], -1)
        plane_ref[10 + 2 * j + 1] = NB * three + kb_ref[at]


def tables(place, far_list, far_count):
    return pl.pallas_call(
        table_body,
        in_specs=[smem(), smem(), smem()],
        out_specs=[smem(), smem(), smem(), smem()],
        out_shape=[
            jax.ShapeDtypeStruct((4, 128), i32),
            jax.ShapeDtypeStruct((64,), i32),
            jax.ShapeDtypeStruct((MID,), i32),
            jax.ShapeDtypeStruct((16,), i32),
        ],
        scratch_shapes=[pltpu.SMEM((128,), i32), pltpu.SMEM((128,), i32)],
        name="tables",
    )(place, far_list, far_count)


def lane_rates():
    rates = []
    for width in (RT, RH, RW):
        rates.append(np.float32(THETA) ** (np.float32(-2.0) * np.arange(width // 2, dtype=np.float32) / np.float32(width)))
    return np.repeat(np.concatenate(rates), 2)[None].astype(np.float32)


def turn_tables(frame, chunk, rates):
    lane = lax.broadcasted_iota(i32, (CH, DH), 1)
    token = lax.broadcasted_iota(i32, (CH, DH), 0)
    below = (token >= FW).astype(i32)
    position = jnp.where(lane < RT, frame, jnp.where(lane < RT + RH, 2 * chunk + below, token - FW * below))
    angle = position.astype(jnp.float32) * rates
    even = lane % 2 == 0
    sine = jnp.sin(angle)
    return jnp.cos(angle), jnp.where(even, -sine, sine), even


def turn(x, tables_):
    cosine, sine, even = tables_
    swapped = jnp.where(even, pltpu.roll(x, DH - 1, 1), pltpu.roll(x, 1, 1))
    return x * cosine + swapped * sine


def enter_kv_body(rows, place_ref, rates_ref, k_ref, v_ref, o_ref, ks, vs):
    tabs = turn_tables(place_ref[2], place_ref[3], rates_ref[...])
    ks[...] = k_ref[...].astype(jnp.float32).reshape(CH * HEADS, DH)
    vs[...] = v_ref[...].astype(jnp.float32).reshape(CH * HEADS, DH)
    for hd in range(8):
        for at, row in enumerate(rows):
            pick = pl.ds(hd * PER + row, CH, stride=HEADS)
            turned = turn(ks[pick, :], tabs).astype(jnp.bfloat16)
            kept = vs[pick, :].astype(jnp.bfloat16)
            for yh in range(2):
                o_ref[yh, hd, at, 0] = turned
                o_ref[yh, hd, at, 1] = kept


def enter_kv(place, rates, key, value, rows):
    return pl.pallas_call(
        lambda *refs: enter_kv_body(rows, *refs),
        in_specs=[smem()] + [pl.BlockSpec(memory_space=pltpu.VMEM)] * 3,
        out_specs=pl.BlockSpec(memory_space=pltpu.VMEM),
        out_shape=jax.ShapeDtypeStruct((2, 8, len(rows), 2, CH, DH), jnp.bfloat16),
        scratch_shapes=[pltpu.VMEM((CH * HEADS, DH), jnp.float32)] * 2,
        compiler_params=params(),
        name="enter_kv",
    )(place, rates, key, value)


def enter_q_body(rows, place_ref, rates_ref, q_ref, o_ref, qs):
    tabs = turn_tables(place_ref[2], place_ref[3], rates_ref[...])
    qs[...] = q_ref[...].astype(jnp.float32).reshape(CH * HEADS, DH)
    for hd in range(8):
        for at, row in enumerate(rows):
            pick = pl.ds(hd * PER + row, CH, stride=HEADS)
            o_ref[hd, at] = turn(qs[pick, :], tabs).astype(jnp.bfloat16)


def enter_q(place, rates, query, rows):
    return pl.pallas_call(
        lambda *refs: enter_q_body(rows, *refs),
        in_specs=[smem()] + [pl.BlockSpec(memory_space=pltpu.VMEM)] * 2,
        out_specs=pl.BlockSpec(memory_space=pltpu.VMEM),
        out_shape=jax.ShapeDtypeStruct((8, len(rows), CH, DH), jnp.bfloat16),
        scratch_shapes=[pltpu.VMEM((CH * HEADS, DH), jnp.float32)],
        compiler_params=params(),
        name="enter_q",
    )(place, rates, query)


def pack_body(place_ref, ask1, ask2, ask3, own_ref, sib_ref, big_ref, mid_ref, out1, out2, out3, frames):
    z, r, c = place_ref[0], place_ref[1], place_ref[4]
    for b in range(2):
        for ref, core in ((own_ref, c), (sib_ref, 1 - c)):
            start = pl.multiple_of((2 * b + core) * TOK, TOK)
            frames[pl.ds(start, TOK), :] = ref[b, :, 0, 0].reshape(TOK, DH)

    def block(index):
        return frames[pl.ds(pl.multiple_of(index * BLK, BLK), BLK), :]

    for s in range(BIG + MID):
        index = jnp.where(r < 2, ask1[z, BESIDE + s], ask3[z, BESIDE + s])
        if s < BIG:
            big_ref[s, 0, 0] = block(index)
        else:
            mid_ref[s - BIG, 0, 0] = block(index)
    for ask, ref in ((ask1, out1), (ask2, out2), (ask3, out3)):
        for s in range(ref.shape[0]):
            ref[s, 0, 0] = block(ask[z, s])


def pack(place, asked, own, sib):
    nh = own.shape[2]
    whole = pl.BlockSpec((2, 8, 1, 1, CH, DH), lambda h, kv: (0, 0, h, kv, 0, 0))

    def out(n):
        return pl.BlockSpec((n, 1, 1, BLK, DH), lambda h, kv: (0, h, kv, 0, 0))

    sizes = (BIG, MID, BESIDE, BASE, BESIDE)
    return pl.pallas_call(
        pack_body,
        grid=(nh, 2),
        in_specs=[smem()] * 4 + [whole, whole],
        out_specs=[out(n) for n in sizes],
        out_shape=[jax.ShapeDtypeStruct((n, nh, 2, BLK, DH), jnp.bfloat16) for n in sizes],
        scratch_shapes=[pltpu.VMEM((PLANE * TOK, DH), jnp.bfloat16)],
        compiler_params=params(),
        name="pack",
    )(place, *asked, own, sib)


def dot_t(a, b):
    return lax.dot_general(a, b, (((1,), (1,)), ((), ())), preferred_element_type=jnp.float32)


def lane_sum(p):
    total = p[:, :DH]
    for at in range(DH, p.shape[1], DH):
        total = total + p[:, at : at + DH]
    return total


def by_lane(op, x):
    total = x[:, :DH]
    for at in range(DH, x.shape[1], DH):
        total = op(total, x[:, at : at + DH])
    return total


def listed_pairs(pairs, qs, m, l, acc, top, scores):
    def rows_of(block):
        return pl.ds(pl.multiple_of(jnp.maximum(block, 0) * BLK, BLK), BLK)

    top[...] = m[...]
    for n, (block, k, _) in enumerate(pairs):
        rows = rows_of(block)
        s = jnp.where(block >= 0, dot_t(qs[rows, :], k()) * SCALE, NONE)
        scores[n] = s
        top[rows, :] = jnp.maximum(top[rows, :], s)
    m_new = jnp.broadcast_to(jnp.max(top[...], axis=1, keepdims=True), (TOK, DH))
    fade = jnp.exp2(m[...] - m_new)
    acc[...] = acc[...] * fade
    l[...] = l[...] * fade
    m[...] = m_new
    for n, (block, _, v) in enumerate(pairs):
        rows = rows_of(block)
        p = jnp.exp2(scores[n] - m[rows, :])
        l[rows, :] += p
        acc[rows, :] += jnp.dot(p.astype(jnp.bfloat16), v(), preferred_element_type=jnp.float32)


QT = 256
NONE = -1e30


def near_body(place_ref, plane_ref, q_ref, own_ref, sib_ref, acc_ref, m_ref, l_ref, qs, kf, vf, top, scores):
    r, c = place_ref[1], place_ref[4]
    qs[...] = q_ref[:, 0].reshape(TOK, DH)
    for b in range(2):
        for ref, core in ((own_ref, c), (sib_ref, 1 - c)):
            start = pl.multiple_of((2 * b + core) * TOK, TOK)
            kf[pl.ds(start, TOK), :] = ref[b, :, 0, 0].reshape(TOK, DH)
            vf[pl.ds(start, TOK), :] = ref[b, :, 0, 1].reshape(TOK, DH)
    acc, m, l = acc_ref.at[0], m_ref.at[0], l_ref.at[0]

    def part(index, size):
        return pl.ds(pl.multiple_of(index * size, size), size)

    third = (r > 0) & (r < PLANE - 1)
    frames = [part(i, TOK) for i in (r, jnp.where(r == 0, 1, r - 1), jnp.where(third, r + 1, r))]

    def tile(t, carry):
        rows = part(t, QT)
        q = qs[rows, :]
        scored = [dot_t(q, kf[at, :]) * SCALE for at in frames]
        scored[2] = jnp.where(third, scored[2], NONE)
        tops = [by_lane(jnp.maximum, s) for s in scored]
        best = jnp.max(jnp.maximum(jnp.maximum(tops[0], tops[1]), tops[2]), axis=1, keepdims=True)
        total = mixed = 0.0
        for s, at in zip(scored, frames, strict=True):
            p = jnp.exp2(s - best)
            total = total + by_lane(jnp.add, p)
            mixed = mixed + jnp.dot(p.astype(jnp.bfloat16), vf[at, :], preferred_element_type=jnp.float32)
        m[rows, :] = jnp.broadcast_to(best, (QT, DH))
        l[rows, :] = total
        acc[rows, :] = mixed
        return carry

    lax.fori_loop(0, TOK // QT, tile, jnp.int32(0))

    def pair(p):
        at = part(plane_ref[2 * p + 1], BLK)
        return plane_ref[2 * p], lambda: kf[at, :], lambda: vf[at, :]

    listed_pairs([pair(p) for p in range(8)], qs, m, l, acc, top, scores)


def head_specs(first):
    tokens = pl.BlockSpec((8, 1, CH, DH), lambda h: (0, h + first if first else h, 0, 0))
    state = pl.BlockSpec((1, TOK, DH), lambda h: (h, 0, 0))
    return tokens, state


def state_shapes(nh):
    return [jax.ShapeDtypeStruct((nh, TOK, DH), jnp.float32)] * 3


def near(place, plane_pairs, q, own, sib, first):
    nh = own.shape[2]
    frames = pl.BlockSpec((2, 8, 1, 2, CH, DH), lambda h: (0, 0, h, 0, 0, 0))
    tokens, state = head_specs(first)
    return pl.pallas_call(
        near_body,
        grid=(nh,),
        in_specs=[smem(), smem(), tokens, frames, frames],
        out_specs=[state] * 3,
        out_shape=state_shapes(nh),
        scratch_shapes=[
            pltpu.VMEM((TOK, DH), jnp.bfloat16),
            pltpu.VMEM((PLANE * TOK, DH), jnp.bfloat16),
            pltpu.VMEM((PLANE * TOK, DH), jnp.bfloat16),
            pltpu.VMEM((TOK, DH), jnp.float32),
            pltpu.VMEM((8, BLK, BLK), jnp.float32),
        ],
        compiler_params=params(),
        name="near",
    )(place, plane_pairs, q, own, sib)


def cross_body(place_ref, q_ref, big_ref, acc_in, m_in, l_in, acc_ref, m_ref, l_ref):
    z, r = place_ref[0], place_ref[1]
    touches = ((r == 0) & (z > 0)) | ((r == PLANE - 1) & (z < 3))

    @pl.when(touches)
    def _():
        k = big_ref[:NB, 0, 0].reshape(TOK, DH)
        v = big_ref[:NB, 0, 1].reshape(TOK, DH)
        q = q_ref[:, 0].reshape(TOK, DH)
        for t in range(TOK // QT):
            rows = slice(t * QT, (t + 1) * QT)
            s = dot_t(q[rows], k) * SCALE
            m_old = m_in[0, rows]
            m_new = jnp.maximum(m_old, jnp.max(by_lane(jnp.maximum, s), axis=1, keepdims=True))
            p = jnp.exp2(s - m_new[:, :1])
            fade = jnp.exp2(m_old - m_new)
            m_ref[0, rows] = m_new
            l_ref[0, rows] = l_in[0, rows] * fade + by_lane(jnp.add, p)
            mixed = jnp.dot(p.astype(jnp.bfloat16), v, preferred_element_type=jnp.float32)
            acc_ref[0, rows] = acc_in[0, rows] * fade + mixed

    @pl.when(jnp.logical_not(touches))
    def _():
        acc_ref[...] = acc_in[...]
        m_ref[...] = m_in[...]
        l_ref[...] = l_in[...]


def cross(place, q, big, state, first):
    nh = big.shape[1]
    tokens, held = head_specs(first)
    blocks = pl.BlockSpec((BIG, 1, 2, BLK, DH), lambda h: (0, h, 0, 0, 0))
    return pl.pallas_call(
        cross_body,
        grid=(nh,),
        in_specs=[smem(), tokens, blocks, held, held, held],
        out_specs=[held] * 3,
        out_shape=state_shapes(nh),
        compiler_params=params(),
        name="cross",
    )(place, q, big, *state)


def far_body(
    place_ref, qslot_ref, late_ref, q_ref, acc_in, m_in, l_in, in1, in2, in3, big_ref, mid_ref, o_ref, qs, acc, m, l, top, scores
):
    z, r = place_ref[0], place_ref[1]
    qs[...] = q_ref[:, 0].reshape(TOK, DH)
    acc[...] = acc_in[0]
    m[...] = m_in[0]
    l[...] = l_in[0]
    pairs = []
    for shift, ref in ((1, in1), (2, in2), (3, in3)):
        zp = (z + 4 - shift) % 4
        for s in range(ref.shape[0]):
            block = qslot_ref[zp * BESIDE + s]
            pairs.append((block, lambda ref=ref, s=s: ref[s, 0, 0], lambda ref=ref, s=s: ref[s, 0, 1]))
    outer = (r == 0) | (r == PLANE - 1)
    for s in range(MID):

        def either(kv, s=s):
            return jnp.where(outer, big_ref[NB, 0, kv], mid_ref[s, 0, kv])

        pairs.append((late_ref[s], lambda either=either: either(0), lambda either=either: either(1)))
    listed_pairs(pairs, qs, m, l, acc, top, scores)
    total = jnp.sum(l[...], axis=1, keepdims=True)
    o_ref[:, 0] = (acc[...] / total).astype(jnp.bfloat16).reshape(8, CH, DH)


def far(place, qslot, late, q, state, crossed, first):
    nh = crossed[0].shape[1]
    tokens, held = head_specs(first)
    blocks = [pl.BlockSpec((x.shape[0], 1, 2, BLK, DH), lambda h: (0, h, 0, 0, 0)) for x in crossed]
    return pl.pallas_call(
        far_body,
        grid=(nh,),
        in_specs=[smem(), smem(), smem(), tokens, held, held, held] + blocks,
        out_specs=pl.BlockSpec((8, 1, CH, DH), lambda h: (0, h, 0, 0)),
        out_shape=jax.ShapeDtypeStruct((8, nh, CH, DH), jnp.bfloat16),
        scratch_shapes=[pltpu.VMEM((TOK, DH), jnp.bfloat16)]
        + [pltpu.VMEM((TOK, DH), jnp.float32)] * 4
        + [pltpu.VMEM((2 * BESIDE + BASE + MID, BLK, BLK), jnp.float32)],
        compiler_params=params(),
        name="far",
    )(place, qslot, late, q, *state, *crossed)


def leave_body(groups, *refs):
    *in_refs, o_ref, s = refs
    for ref, rows in zip(in_refs, groups, strict=True):
        for hd in range(8):
            for at, row in enumerate(rows):
                s[pl.ds(hd * PER + row, CH, stride=HEADS), :] = ref[hd, at].astype(jnp.float32)
    o_ref[...] = s[...].reshape(CH, HEADS, DH).astype(jnp.bfloat16)


def leave(parts, groups):
    return pl.pallas_call(
        lambda *refs: leave_body(groups, *refs),
        in_specs=[pl.BlockSpec(memory_space=pltpu.VMEM)] * len(parts),
        out_specs=pl.BlockSpec(memory_space=pltpu.VMEM),
        out_shape=jax.ShapeDtypeStruct((CH, HEADS, DH), jnp.bfloat16),
        scratch_shapes=[pltpu.VMEM((CH * HEADS, DH), jnp.float32)],
        compiler_params=params(),
        name="leave",
    )(*parts)


def at_plane(z, r):
    return PLANE * z + r


TM = ("z", "yh", "c")
BIG_PAIRS = [(at_plane(z, 0), at_plane(z + 1, 0)) for z in range(3)] + [(at_plane(z + 1, 3), at_plane(z, 3)) for z in range(3)]

MID_PAIRS = [(at_plane(z, 1), at_plane(z + 1, 1)) for z in range(3)] + [(at_plane(z + 1, 2), at_plane(z, 2)) for z in range(3)]


def together(*values):
    return lax.optimization_barrier(values)


def shards(query, key, value, far_list, far_count):
    z, yh, c, hd = (lax.axis_index(a) for a in ("z", "yh", "c", "head"))
    r = 2 * yh + c
    place = jnp.stack([z, r, PLANE * z + r, hd, c]).astype(i32)
    rates = jnp.asarray(lane_rates())
    first, rest = CHUNKS
    a_at, b_at = first[0], rest[0]

    def around(x, shift):
        return lax.ppermute(x, "z", [(i, (i + shift) % 4) for i in range(4)])

    def entry(sent):
        nh = sent.shape[2]
        own = lax.all_to_all(sent.reshape(16, nh, 2, CH, DH), ("yh", "head"), 0, 0, tiled=True)
        return own.reshape(2, 8, nh, 2, CH, DH)

    def swap(x):
        return lax.ppermute(x, "c", [(0, 1), (1, 0)])

    def by_head(x):
        return lax.all_to_all(x, "head", 0, 0, tiled=True)

    def send(packed):
        big, mid, *base = packed
        big = lax.ppermute(big, TM, BIG_PAIRS)
        base = [around(x, shift) for shift, x in zip((1, 2, 3), base, strict=True)]
        return [*base, big, lax.ppermute(mid, TM, MID_PAIRS)]

    sent_a = enter_kv(place, rates, key, value, first)
    far_list, key, value, query, sent_a = together(far_list, key, value, query, sent_a)
    want, qslot, late, plane_pairs = tables(place, far_list, far_count)
    asked = [around(want, -shift) for shift in (1, 2, 3)]
    sent_b = enter_kv(place, rates, key, value, rest)
    sent_q = enter_q(place, rates, query, first + rest)
    own_a = entry(sent_a)
    own_a, sent_b, sent_q, asked = together(own_a, sent_b, sent_q, asked)
    sib_a = swap(own_a)
    own_b = entry(sent_b)
    packed_a = pack(place, asked, own_a, sib_a)
    crossed_a = send(packed_a)
    own_b, sent_q, crossed_a = together(own_b, sent_q, crossed_a)
    sib_b = swap(own_b)
    q = by_head(sent_q)
    packed_b = pack(place, asked, own_b, sib_b)
    crossed_b = send(packed_b)
    q, _ = together(q, packed_b)
    state_a = near(place, plane_pairs, q, own_a, sib_a, a_at)
    state_a = cross(place, q, crossed_a[3], state_a, a_at)
    done_a = far(place, qslot, late, q, state_a, crossed_a, a_at)
    out_a = by_head(done_a)
    q, _ = together(q, done_a)
    state_b = near(place, plane_pairs, q, own_b, sib_b, b_at)
    state_b = cross(place, q, crossed_b[3], state_b, b_at)
    out_b = by_head(far(place, qslot, late, q, state_b, crossed_b, b_at))
    return leave((out_a, out_b), CHUNKS)


def solution(mesh):
    split = Mesh(mesh.devices.reshape(4, 2, 2, 8), ("z", "yh", "c", "head"))
    tokens = P(("z", "yh", "c", "head"), None, None)
    blocks = P(TM, None)
    return jax.shard_map(
        shards,
        mesh=split,
        in_specs=(tokens, tokens, tokens, blocks, blocks),
        out_specs=tokens,
        check_vma=False,
    )
```

```python
import jax
import jax.numpy as jnp
import numpy as np
from jax import lax
from jax.experimental import pallas as pl
from jax.experimental.pallas import tpu as pltpu
from jax.sharding import Mesh
from jax.sharding import PartitionSpec as P

FW = 80
TOK = 1280
BLK = 128
CH = 160
NB = 10
DH = 128
RT, RH, RW = 16, 56, 56
HEADS = 24
PER = 3
PLANE = 4
THETA = 256.0
SCALE = float(DH**-0.5 * np.log2(np.e))
CHUNKS = ((0,), (1, 2))

BASE = 8
BESIDE = 12
BIG = 8
VMEM = 58 * 2**20

i32 = jnp.int32


def params():
    return pltpu.CompilerParams(vmem_limit_bytes=VMEM)


def smem():
    return pl.BlockSpec(memory_space=pltpu.SMEM)


def table_body(place_ref, list_ref, count_ref, want_ref, qslot_ref, plane_ref, kb_ref, qb_ref):
    z, r = place_ref[0], place_ref[1]
    f = PLANE * z + r

    def frame_lists(g, carry):
        for j in range(8):
            kb_ref[g * 8 + j] = 0
            qb_ref[g * 8 + j] = 0

        def one_block(n, filled):
            kb_ref[g * 8 + filled] = list_ref[n, g] - NB * g
            qb_ref[g * 8 + filled] = n
            return filled + jnp.where(count_ref[n, g] > 0, 1, 0).astype(i32)

        lax.fori_loop(0, NB, one_block, jnp.int32(0))
        return carry

    lax.fori_loop(0, PLANE * 4, frame_lists, jnp.int32(0))

    def clear(s, carry):
        for zp in range(4):
            want_ref[zp, s] = 0
        return carry

    lax.fori_loop(0, 128, clear, jnp.int32(0))
    for s in range(64):
        qslot_ref[s] = -1
    for zp in range(4):
        for i in range(PLANE):
            g = PLANE * zp + i
            far = jnp.abs(f - g) >= 2
            for j in range(2):
                want_ref[zp, 2 * i + j] = NB * i + kb_ref[g * 8 + j]
                qslot_ref[zp * BESIDE + 2 * i + j] = jnp.where(far & (z != zp), qb_ref[g * 8 + j], -1)

    def listed(zp, s, i, j):
        at = (PLANE * zp + i) * 8 + j
        want_ref[zp, s] = NB * i + kb_ref[at]
        qslot_ref[zp * BESIDE + s] = qb_ref[at]

    def side(up, first, second, third):
        zp = z - 1 if up else z + 1
        exists = z > 0 if up else z < 3
        near, two, three = (3, 2, 1) if up else (0, 1, 2)

        @pl.when(exists & (r == first))
        def _():
            for j in range(2):
                listed(zp, 2 * near + j, two, 2 + j)
            listed(zp, BASE, two, 4)
            listed(zp, BESIDE - 1, three, 2)
            for n in range(BIG):
                want_ref[zp, BESIDE + n] = NB * near + n
            for n in range(BIG, NB):
                want_ref[zp, BASE + 1 + n - BIG] = NB * near + n

        @pl.when(exists & (r == second))
        def _():
            listed(zp, BASE, two, 2)
            for j in range(3):
                listed(zp, BASE + 1 + j, near, 2 + j)

        @pl.when(exists & (r == third))
        def _():
            listed(zp, BASE, near, 2)

    side(True, 0, 1, 2)
    side(False, 3, 2, 1)

    two = (r + 2) % PLANE
    three = PLANE - 1 - r
    outer = (r == 0) | (r == PLANE - 1)
    for j in range(5):
        at = (PLANE * z + two) * 8 + j
        plane_ref[2 * j] = qb_ref[at]
        plane_ref[2 * j + 1] = NB * two + kb_ref[at]
    for j in range(3):
        at = (PLANE * z + three) * 8 + j
        plane_ref[10 + 2 * j] = jnp.where(outer, qb_ref[at], -1)
        plane_ref[10 + 2 * j + 1] = NB * three + kb_ref[at]


def tables(place, far_list, far_count):
    return pl.pallas_call(
        table_body,
        in_specs=[smem(), smem(), smem()],
        out_specs=[smem(), smem(), smem()],
        out_shape=[
            jax.ShapeDtypeStruct((4, 128), i32),
            jax.ShapeDtypeStruct((64,), i32),
            jax.ShapeDtypeStruct((16,), i32),
        ],
        scratch_shapes=[pltpu.SMEM((128,), i32), pltpu.SMEM((128,), i32)],
        name="tables",
    )(place, far_list, far_count)


def lane_rates():
    rates = []
    for width in (RT, RH, RW):
        rates.append(np.float32(THETA) ** (np.float32(-2.0) * np.arange(width // 2, dtype=np.float32) / np.float32(width)))
    return np.repeat(np.concatenate(rates), 2)[None].astype(np.float32)


def turn_tables(frame, chunk, rates):
    lane = lax.broadcasted_iota(i32, (CH, DH), 1)
    token = lax.broadcasted_iota(i32, (CH, DH), 0)
    below = (token >= FW).astype(i32)
    position = jnp.where(lane < RT, frame, jnp.where(lane < RT + RH, 2 * chunk + below, token - FW * below))
    angle = position.astype(jnp.float32) * rates
    even = lane % 2 == 0
    sine = jnp.sin(angle)
    return jnp.cos(angle), jnp.where(even, -sine, sine), even


def turn(x, tables_):
    cosine, sine, even = tables_
    swapped = jnp.where(even, pltpu.roll(x, DH - 1, 1), pltpu.roll(x, 1, 1))
    return x * cosine + swapped * sine


def enter_kv_body(rows, place_ref, rates_ref, k_ref, v_ref, o_ref, ks, vs):
    tabs = turn_tables(place_ref[2], place_ref[3], rates_ref[...])
    ks[...] = k_ref[...].astype(jnp.float32).reshape(CH * HEADS, DH)
    vs[...] = v_ref[...].astype(jnp.float32).reshape(CH * HEADS, DH)
    for hd in range(8):
        for at, row in enumerate(rows):
            pick = pl.ds(hd * PER + row, CH, stride=HEADS)
            turned = turn(ks[pick, :], tabs).astype(jnp.bfloat16)
            kept = vs[pick, :].astype(jnp.bfloat16)
            for yh in range(2):
                o_ref[yh, hd, at, 0] = turned
                o_ref[yh, hd, at, 1] = kept


def enter_kv(place, rates, key, value, rows):
    return pl.pallas_call(
        lambda *refs: enter_kv_body(rows, *refs),
        in_specs=[smem()] + [pl.BlockSpec(memory_space=pltpu.VMEM)] * 3,
        out_specs=pl.BlockSpec(memory_space=pltpu.VMEM),
        out_shape=jax.ShapeDtypeStruct((2, 8, len(rows), 2, CH, DH), jnp.bfloat16),
        scratch_shapes=[pltpu.VMEM((CH * HEADS, DH), jnp.float32)] * 2,
        compiler_params=params(),
        name="enter_kv",
    )(place, rates, key, value)


def enter_q_body(rows, place_ref, rates_ref, q_ref, o_ref, qs):
    tabs = turn_tables(place_ref[2], place_ref[3], rates_ref[...])
    qs[...] = q_ref[...].astype(jnp.float32).reshape(CH * HEADS, DH)
    for hd in range(8):
        for at, row in enumerate(rows):
            pick = pl.ds(hd * PER + row, CH, stride=HEADS)
            o_ref[hd, at] = turn(qs[pick, :], tabs).astype(jnp.bfloat16)


def enter_q(place, rates, query, rows):
    return pl.pallas_call(
        lambda *refs: enter_q_body(rows, *refs),
        in_specs=[smem()] + [pl.BlockSpec(memory_space=pltpu.VMEM)] * 2,
        out_specs=pl.BlockSpec(memory_space=pltpu.VMEM),
        out_shape=jax.ShapeDtypeStruct((8, len(rows), CH, DH), jnp.bfloat16),
        scratch_shapes=[pltpu.VMEM((CH * HEADS, DH), jnp.float32)],
        compiler_params=params(),
        name="enter_q",
    )(place, rates, query)


def pack_body(place_ref, ask1, ask2, ask3, own_ref, sib_ref, big_ref, out1, out2, out3, frames):
    z, r, c = place_ref[0], place_ref[1], place_ref[4]
    for b in range(2):
        for ref, core in ((own_ref, c), (sib_ref, 1 - c)):
            start = pl.multiple_of((2 * b + core) * TOK, TOK)
            frames[pl.ds(start, TOK), :] = ref[b, :, 0, 0].reshape(TOK, DH)

    def block(index):
        return frames[pl.ds(pl.multiple_of(index * BLK, BLK), BLK), :]

    for s in range(BIG):
        big_ref[s, 0, 0] = block(jnp.where(r < 2, ask1[z, BESIDE + s], ask3[z, BESIDE + s]))
    for ask, ref in ((ask1, out1), (ask2, out2), (ask3, out3)):
        for s in range(ref.shape[0]):
            ref[s, 0, 0] = block(ask[z, s])


def pack(place, asked, own, sib):
    nh = own.shape[2]
    whole = pl.BlockSpec((2, 8, 1, 1, CH, DH), lambda h, kv: (0, 0, h, kv, 0, 0))

    def out(n):
        return pl.BlockSpec((n, 1, 1, BLK, DH), lambda h, kv: (0, h, kv, 0, 0))

    sizes = (BIG, BESIDE, BASE, BESIDE)
    return pl.pallas_call(
        pack_body,
        grid=(nh, 2),
        in_specs=[smem()] * 4 + [whole, whole],
        out_specs=[out(n) for n in sizes],
        out_shape=[jax.ShapeDtypeStruct((n, nh, 2, BLK, DH), jnp.bfloat16) for n in sizes],
        scratch_shapes=[pltpu.VMEM((PLANE * TOK, DH), jnp.bfloat16)],
        compiler_params=params(),
        name="pack",
    )(place, *asked, own, sib)


def dot_t(a, b):
    return lax.dot_general(a, b, (((1,), (1,)), ((), ())), preferred_element_type=jnp.float32)


def lane_sum(p):
    total = p[:, :DH]
    for at in range(DH, p.shape[1], DH):
        total = total + p[:, at : at + DH]
    return total


def by_lane(op, x):
    total = x[:, :DH]
    for at in range(DH, x.shape[1], DH):
        total = op(total, x[:, at : at + DH])
    return total


def listed_pairs(pairs, qs, m, l, acc, top, scores):
    def rows_of(block):
        return pl.ds(pl.multiple_of(jnp.maximum(block, 0) * BLK, BLK), BLK)

    top[...] = m[...]
    for n, (block, k, _) in enumerate(pairs):
        rows = rows_of(block)
        s = jnp.where(block >= 0, dot_t(qs[rows, :], k()) * SCALE, NONE)
        scores[n] = s
        top[rows, :] = jnp.maximum(top[rows, :], s)
    m_new = jnp.broadcast_to(jnp.max(top[...], axis=1, keepdims=True), (TOK, DH))
    fade = jnp.exp2(m[...] - m_new)
    acc[...] = acc[...] * fade
    l[...] = l[...] * fade
    m[...] = m_new
    for n, (block, _, v) in enumerate(pairs):
        rows = rows_of(block)
        p = jnp.exp2(scores[n] - m[rows, :])
        l[rows, :] += p
        acc[rows, :] += jnp.dot(p.astype(jnp.bfloat16), v(), preferred_element_type=jnp.float32)


QT = 256
NONE = -1e30


def near_body(place_ref, plane_ref, q_ref, own_ref, sib_ref, acc_ref, m_ref, l_ref, qs, kf, vf, top, scores):
    r, c = place_ref[1], place_ref[4]
    qs[...] = q_ref[:, 0].reshape(TOK, DH)
    for b in range(2):
        for ref, core in ((own_ref, c), (sib_ref, 1 - c)):
            start = pl.multiple_of((2 * b + core) * TOK, TOK)
            kf[pl.ds(start, TOK), :] = ref[b, :, 0, 0].reshape(TOK, DH)
            vf[pl.ds(start, TOK), :] = ref[b, :, 0, 1].reshape(TOK, DH)
    acc, m, l = acc_ref.at[0], m_ref.at[0], l_ref.at[0]

    def part(index, size):
        return pl.ds(pl.multiple_of(index * size, size), size)

    third = (r > 0) & (r < PLANE - 1)
    frames = [part(i, TOK) for i in (r, jnp.where(r == 0, 1, r - 1), jnp.where(third, r + 1, r))]

    def tile(t, carry):
        rows = part(t, QT)
        q = qs[rows, :]
        scored = [dot_t(q, kf[at, :]) * SCALE for at in frames]
        scored[2] = jnp.where(third, scored[2], NONE)
        tops = [by_lane(jnp.maximum, s) for s in scored]
        best = jnp.max(jnp.maximum(jnp.maximum(tops[0], tops[1]), tops[2]), axis=1, keepdims=True)
        total = mixed = 0.0
        for s, at in zip(scored, frames, strict=True):
            p = jnp.exp2(s - best)
            total = total + by_lane(jnp.add, p)
            mixed = mixed + jnp.dot(p.astype(jnp.bfloat16), vf[at, :], preferred_element_type=jnp.float32)
        m[rows, :] = jnp.broadcast_to(best, (QT, DH))
        l[rows, :] = total
        acc[rows, :] = mixed
        return carry

    lax.fori_loop(0, TOK // QT, tile, jnp.int32(0))

    def pair(p):
        at = part(plane_ref[2 * p + 1], BLK)
        return plane_ref[2 * p], lambda: kf[at, :], lambda: vf[at, :]

    listed_pairs([pair(p) for p in range(8)], qs, m, l, acc, top, scores)


def head_specs(at=0):
    tokens = pl.BlockSpec((8, 1, CH, DH), lambda h: (0, h + at if at else h, 0, 0))
    state = pl.BlockSpec((1, TOK, DH), lambda h: (h, 0, 0))
    return tokens, state


def state_shapes(nh):
    return [jax.ShapeDtypeStruct((nh, TOK, DH), jnp.float32)] * 3


def near(place, plane_pairs, q, own, sib, at):
    nh = own.shape[2]
    frames = pl.BlockSpec((2, 8, 1, 2, CH, DH), lambda h: (0, 0, h, 0, 0, 0))
    tokens, state = head_specs(at)
    return pl.pallas_call(
        near_body,
        grid=(nh,),
        in_specs=[smem(), smem(), tokens, frames, frames],
        out_specs=[state] * 3,
        out_shape=state_shapes(nh),
        scratch_shapes=[
            pltpu.VMEM((TOK, DH), jnp.bfloat16),
            pltpu.VMEM((PLANE * TOK, DH), jnp.bfloat16),
            pltpu.VMEM((PLANE * TOK, DH), jnp.bfloat16),
            pltpu.VMEM((TOK, DH), jnp.float32),
            pltpu.VMEM((8, BLK, BLK), jnp.float32),
        ],
        compiler_params=params(),
        name="near",
    )(place, plane_pairs, q, own, sib)


def cross_body(place_ref, q_ref, big_ref, in1, in3, acc_in, m_in, l_in, acc_ref, m_ref, l_ref, kf, vf):
    z, r = place_ref[0], place_ref[1]
    touches = ((r == 0) & (z > 0)) | ((r == PLANE - 1) & (z < 3))

    @pl.when(touches)
    def _():
        for kv, ref in ((0, kf), (1, vf)):
            ref[: BIG * BLK] = big_ref[:, 0, kv].reshape(BIG * BLK, DH)
            for n in range(BIG, NB):
                s = BASE + 1 + n - BIG
                ref[n * BLK : (n + 1) * BLK] = jnp.where(r == 0, in1[s, 0, kv], in3[s, 0, kv])
        q = q_ref[:, 0].reshape(TOK, DH)
        for t in range(TOK // QT):
            rows = slice(t * QT, (t + 1) * QT)
            s = dot_t(q[rows], kf[...]) * SCALE
            m_old = m_in[0, rows]
            m_new = jnp.maximum(m_old, jnp.max(by_lane(jnp.maximum, s), axis=1, keepdims=True))
            p = jnp.exp2(s - m_new[:, :1])
            fade = jnp.exp2(m_old - m_new)
            m_ref[0, rows] = m_new
            l_ref[0, rows] = l_in[0, rows] * fade + by_lane(jnp.add, p)
            mixed = jnp.dot(p.astype(jnp.bfloat16), vf[...], preferred_element_type=jnp.float32)
            acc_ref[0, rows] = acc_in[0, rows] * fade + mixed

    @pl.when(jnp.logical_not(touches))
    def _():
        acc_ref[...] = acc_in[...]
        m_ref[...] = m_in[...]
        l_ref[...] = l_in[...]


def block_specs(arrays):
    return [pl.BlockSpec((x.shape[0], 1, 2, BLK, DH), lambda h: (0, h, 0, 0, 0)) for x in arrays]


def cross(place, q, big, in1, in3, state, at):
    nh = big.shape[1]
    tokens, held = head_specs(at)
    return pl.pallas_call(
        cross_body,
        grid=(nh,),
        in_specs=[smem(), tokens] + block_specs((big, in1, in3)) + [held] * 3,
        out_specs=[held] * 3,
        out_shape=state_shapes(nh),
        scratch_shapes=[pltpu.VMEM((TOK, DH), jnp.bfloat16)] * 2,
        compiler_params=params(),
        name="cross",
    )(place, q, big, in1, in3, *state)


def far_body(place_ref, qslot_ref, q_ref, acc_in, m_in, l_in, in1, in2, in3, o_ref, qs, acc, m, l, top, scores):
    z = place_ref[0]
    qs[...] = q_ref[:, 0].reshape(TOK, DH)
    acc[...] = acc_in[0]
    m[...] = m_in[0]
    l[...] = l_in[0]
    pairs = []
    for shift, ref in ((1, in1), (2, in2), (3, in3)):
        zp = (z + 4 - shift) % 4
        for s in range(ref.shape[0]):
            block = qslot_ref[zp * BESIDE + s]
            pairs.append((block, lambda ref=ref, s=s: ref[s, 0, 0], lambda ref=ref, s=s: ref[s, 0, 1]))
    listed_pairs(pairs, qs, m, l, acc, top, scores)
    total = jnp.sum(l[...], axis=1, keepdims=True)
    o_ref[:, 0] = (acc[...] / total).astype(jnp.bfloat16).reshape(8, CH, DH)


def far(place, qslot, q, state, base, at):
    nh = base[0].shape[1]
    tokens, held = head_specs(at)
    return pl.pallas_call(
        far_body,
        grid=(nh,),
        in_specs=[smem(), smem(), tokens, held, held, held] + block_specs(base),
        out_specs=pl.BlockSpec((8, 1, CH, DH), lambda h: (0, h, 0, 0)),
        out_shape=jax.ShapeDtypeStruct((8, nh, CH, DH), jnp.bfloat16),
        scratch_shapes=[pltpu.VMEM((TOK, DH), jnp.bfloat16)]
        + [pltpu.VMEM((TOK, DH), jnp.float32)] * 4
        + [pltpu.VMEM((2 * BESIDE + BASE, BLK, BLK), jnp.float32)],
        compiler_params=params(),
        name="far",
    )(place, qslot, q, *state, *base)


def leave_body(groups, *refs):
    *in_refs, o_ref, s = refs
    for ref, rows in zip(in_refs, groups, strict=True):
        for hd in range(8):
            for at, row in enumerate(rows):
                s[pl.ds(hd * PER + row, CH, stride=HEADS), :] = ref[hd, at].astype(jnp.float32)
    o_ref[...] = s[...].reshape(CH, HEADS, DH).astype(jnp.bfloat16)


def leave(parts, groups):
    return pl.pallas_call(
        lambda *refs: leave_body(groups, *refs),
        in_specs=[pl.BlockSpec(memory_space=pltpu.VMEM)] * len(parts),
        out_specs=pl.BlockSpec(memory_space=pltpu.VMEM),
        out_shape=jax.ShapeDtypeStruct((CH, HEADS, DH), jnp.bfloat16),
        scratch_shapes=[pltpu.VMEM((CH * HEADS, DH), jnp.float32)],
        compiler_params=params(),
        name="leave",
    )(*parts)


def at_plane(z, r):
    return PLANE * z + r


TM = ("z", "yh", "c")
BIG_PAIRS = [(at_plane(z, 0), at_plane(z + 1, 0)) for z in range(3)] + [(at_plane(z + 1, 3), at_plane(z, 3)) for z in range(3)]


def together(*values):
    return lax.optimization_barrier(values)


def shards(query, key, value, far_list, far_count):
    z, yh, c, hd = (lax.axis_index(a) for a in ("z", "yh", "c", "head"))
    r = 2 * yh + c
    place = jnp.stack([z, r, PLANE * z + r, hd, c]).astype(i32)
    rates = jnp.asarray(lane_rates())
    def around(x, shift):
        return lax.ppermute(x, "z", [(i, (i + shift) % 4) for i in range(4)])

    def entry(sent):
        nh = sent.shape[2]
        own = lax.all_to_all(sent.reshape(16, nh, 2, CH, DH), ("yh", "head"), 0, 0, tiled=True)
        return own.reshape(2, 8, nh, 2, CH, DH)

    def swap(x):
        return lax.ppermute(x, "c", [(0, 1), (1, 0)])

    def by_head(x):
        return lax.all_to_all(x, "head", 0, 0, tiled=True)

    def send(packed):
        big, *base = packed
        big = lax.ppermute(big, TM, BIG_PAIRS)
        return big, *(around(x, shift) for shift, x in zip((1, 2, 3), base, strict=True))

    sent_a = enter_kv(place, rates, key, value, CHUNKS[0])
    far_list, key, value, sent_a = together(far_list, key, value, sent_a)
    want, qslot, plane_pairs = tables(place, far_list, far_count)
    asked = [around(want, -shift) for shift in (1, 2, 3)]
    sent_b = enter_kv(place, rates, key, value, CHUNKS[1])
    own_a = entry(sent_a)
    own_a, sent_b, asked = together(own_a, sent_b, asked)
    own_b = entry(sent_b)
    sib_a = swap(own_a)
    packed_a = pack(place, asked, own_a, sib_a)
    packed_a, query = together(packed_a, query)
    big_a, in1_a, in2_a, in3_a = send(packed_a)
    q_a, q_b = (enter_q(place, rates, query, rows) for rows in CHUNKS)
    own_b, q_a, q_b, big_a, in1_a, in3_a = together(own_b, q_a, q_b, big_a, in1_a, in3_a)
    sib_b = swap(own_b)
    q_a = by_head(q_a)
    packed_b = pack(place, asked, own_b, sib_b)
    packed_b, q_a, in2_a = together(packed_b, q_a, in2_a)
    big_b, in1_b, in2_b, in3_b = send(packed_b)
    q_b = by_head(q_b)
    state_a = near(place, plane_pairs, q_a, own_a, sib_a, 0)
    state_a = cross(place, q_a, big_a, in1_a, in3_a, state_a, 0)
    done_a = far(place, qslot, q_a, state_a, (in1_a, in2_a, in3_a), 0)
    out_a = by_head(done_a)
    q_b, _ = together(q_b, done_a)
    state_b = near(place, plane_pairs, q_b, own_b, sib_b, 0)
    state_b = cross(place, q_b, big_b, in1_b, in3_b, state_b, 0)
    out_b = by_head(far(place, qslot, q_b, state_b, (in1_b, in2_b, in3_b), 0))
    return leave((out_a, out_b), CHUNKS)


def solution(mesh):
    split = Mesh(mesh.devices.reshape(4, 2, 2, 8), ("z", "yh", "c", "head"))
    tokens = P(("z", "yh", "c", "head"), None, None)
    blocks = P(TM, None)
    return jax.shard_map(
        shards,
        mesh=split,
        in_specs=(tokens, tokens, tokens, blocks, blocks),
        out_specs=tokens,
        check_vma=False,
    )
```

```python
import jax
import jax.numpy as jnp
import numpy as np
from jax import lax
from jax.experimental import pallas as pl
from jax.experimental.pallas import tpu as pltpu
from jax.sharding import Mesh
from jax.sharding import PartitionSpec as P

FW = 80
TOK = 1280
BLK = 128
CH = 160
NB = 10
DH = 128
RT, RH, RW = 16, 56, 56
HEADS = 24
PER = 3
PLANE = 4
THETA = 256.0
SCALE = float(DH**-0.5 * np.log2(np.e))
CHUNKS = ((0,), (1, 2))

BASE = 8
BESIDE = 12
BIG = 8
VMEM = 58 * 2**20

i32 = jnp.int32


def params():
    return pltpu.CompilerParams(vmem_limit_bytes=VMEM)


def smem():
    return pl.BlockSpec(memory_space=pltpu.SMEM)


def table_body(place_ref, list_ref, count_ref, want_ref, qslot_ref, plane_ref, kb_ref, qb_ref):
    z, r = place_ref[0], place_ref[1]
    f = PLANE * z + r

    def frame_lists(g, carry):
        for j in range(8):
            kb_ref[g * 8 + j] = 0
            qb_ref[g * 8 + j] = 0

        def one_block(n, filled):
            kb_ref[g * 8 + filled] = list_ref[n, g] - NB * g
            qb_ref[g * 8 + filled] = n
            return filled + jnp.where(count_ref[n, g] > 0, 1, 0).astype(i32)

        lax.fori_loop(0, NB, one_block, jnp.int32(0))
        return carry

    lax.fori_loop(0, PLANE * 4, frame_lists, jnp.int32(0))

    def clear(s, carry):
        for zp in range(4):
            want_ref[zp, s] = 0
        return carry

    lax.fori_loop(0, 128, clear, jnp.int32(0))
    for s in range(64):
        qslot_ref[s] = -1
    for zp in range(4):
        for i in range(PLANE):
            g = PLANE * zp + i
            far = jnp.abs(f - g) >= 2
            for j in range(2):
                want_ref[zp, 2 * i + j] = NB * i + kb_ref[g * 8 + j]
                qslot_ref[zp * BESIDE + 2 * i + j] = jnp.where(far & (z != zp), qb_ref[g * 8 + j], -1)

    def listed(zp, s, i, j):
        at = (PLANE * zp + i) * 8 + j
        want_ref[zp, s] = NB * i + kb_ref[at]
        qslot_ref[zp * BESIDE + s] = qb_ref[at]

    def side(up, first, second, third):
        zp = z - 1 if up else z + 1
        exists = z > 0 if up else z < 3
        near, two, three = (3, 2, 1) if up else (0, 1, 2)

        @pl.when(exists & (r == first))
        def _():
            for j in range(2):
                listed(zp, 2 * near + j, two, 2 + j)
            listed(zp, BASE, two, 4)
            listed(zp, BESIDE - 1, three, 2)
            for n in range(BIG):
                want_ref[zp, BESIDE + n] = NB * near + n
            for n in range(BIG, NB):
                want_ref[zp, BASE + 1 + n - BIG] = NB * near + n

        @pl.when(exists & (r == second))
        def _():
            listed(zp, BASE, two, 2)
            for j in range(3):
                listed(zp, BASE + 1 + j, near, 2 + j)

        @pl.when(exists & (r == third))
        def _():
            listed(zp, BASE, near, 2)

    side(True, 0, 1, 2)
    side(False, 3, 2, 1)

    two = (r + 2) % PLANE
    three = PLANE - 1 - r
    outer = (r == 0) | (r == PLANE - 1)
    for j in range(5):
        at = (PLANE * z + two) * 8 + j
        plane_ref[2 * j] = qb_ref[at]
        plane_ref[2 * j + 1] = NB * two + kb_ref[at]
    for j in range(3):
        at = (PLANE * z + three) * 8 + j
        plane_ref[10 + 2 * j] = jnp.where(outer, qb_ref[at], -1)
        plane_ref[10 + 2 * j + 1] = NB * three + kb_ref[at]


def tables(place, far_list, far_count):
    return pl.pallas_call(
        table_body,
        in_specs=[smem(), smem(), smem()],
        out_specs=[smem(), smem(), smem()],
        out_shape=[
            jax.ShapeDtypeStruct((4, 128), i32),
            jax.ShapeDtypeStruct((64,), i32),
            jax.ShapeDtypeStruct((16,), i32),
        ],
        scratch_shapes=[pltpu.SMEM((128,), i32), pltpu.SMEM((128,), i32)],
        name="tables",
    )(place, far_list, far_count)


def lane_rates():
    rates = []
    for width in (RT, RH, RW):
        rates.append(np.float32(THETA) ** (np.float32(-2.0) * np.arange(width // 2, dtype=np.float32) / np.float32(width)))
    return np.repeat(np.concatenate(rates), 2)[None].astype(np.float32)


def turn_tables(frame, chunk, rates):
    lane = lax.broadcasted_iota(i32, (CH, DH), 1)
    token = lax.broadcasted_iota(i32, (CH, DH), 0)
    below = (token >= FW).astype(i32)
    position = jnp.where(lane < RT, frame, jnp.where(lane < RT + RH, 2 * chunk + below, token - FW * below))
    angle = position.astype(jnp.float32) * rates
    even = lane % 2 == 0
    sine = jnp.sin(angle)
    return jnp.cos(angle), jnp.where(even, -sine, sine), even


def turn(x, tables_):
    cosine, sine, even = tables_
    swapped = jnp.where(even, pltpu.roll(x, DH - 1, 1), pltpu.roll(x, 1, 1))
    return x * cosine + swapped * sine


def enter_kv_body(rows, place_ref, rates_ref, k_ref, v_ref, o_ref, ks, vs):
    tabs = turn_tables(place_ref[2], place_ref[3], rates_ref[...])
    ks[...] = k_ref[...].astype(jnp.float32).reshape(CH * HEADS, DH)
    vs[...] = v_ref[...].astype(jnp.float32).reshape(CH * HEADS, DH)
    for hd in range(8):
        for at, row in enumerate(rows):
            pick = pl.ds(hd * PER + row, CH, stride=HEADS)
            turned = turn(ks[pick, :], tabs).astype(jnp.bfloat16)
            kept = vs[pick, :].astype(jnp.bfloat16)
            for yh in range(2):
                o_ref[yh, hd, at, 0] = turned
                o_ref[yh, hd, at, 1] = kept


def enter_kv(place, rates, key, value, rows):
    return pl.pallas_call(
        lambda *refs: enter_kv_body(rows, *refs),
        in_specs=[smem()] + [pl.BlockSpec(memory_space=pltpu.VMEM)] * 3,
        out_specs=pl.BlockSpec(memory_space=pltpu.VMEM),
        out_shape=jax.ShapeDtypeStruct((2, 8, len(rows), 2, CH, DH), jnp.bfloat16),
        scratch_shapes=[pltpu.VMEM((CH * HEADS, DH), jnp.float32)] * 2,
        compiler_params=params(),
        name="enter_kv",
    )(place, rates, key, value)


def enter_q_body(rows, place_ref, rates_ref, q_ref, o_ref, qs):
    tabs = turn_tables(place_ref[2], place_ref[3], rates_ref[...])
    qs[...] = q_ref[...].astype(jnp.float32).reshape(CH * HEADS, DH)
    for hd in range(8):
        for at, row in enumerate(rows):
            pick = pl.ds(hd * PER + row, CH, stride=HEADS)
            o_ref[hd, at] = turn(qs[pick, :], tabs).astype(jnp.bfloat16)


def enter_q(place, rates, query, rows):
    return pl.pallas_call(
        lambda *refs: enter_q_body(rows, *refs),
        in_specs=[smem()] + [pl.BlockSpec(memory_space=pltpu.VMEM)] * 2,
        out_specs=pl.BlockSpec(memory_space=pltpu.VMEM),
        out_shape=jax.ShapeDtypeStruct((8, len(rows), CH, DH), jnp.bfloat16),
        scratch_shapes=[pltpu.VMEM((CH * HEADS, DH), jnp.float32)],
        compiler_params=params(),
        name="enter_q",
    )(place, rates, query)


def pack_body(place_ref, ask1, ask2, ask3, own_ref, sib_ref, big_ref, out1, out2, out3, frames):
    z, r, c = place_ref[0], place_ref[1], place_ref[4]
    for b in range(2):
        for ref, core in ((own_ref, c), (sib_ref, 1 - c)):
            start = pl.multiple_of((2 * b + core) * TOK, TOK)
            frames[pl.ds(start, TOK), :] = ref[b, :, 0, 0].reshape(TOK, DH)

    def block(index):
        return frames[pl.ds(pl.multiple_of(index * BLK, BLK), BLK), :]

    for s in range(BIG):
        big_ref[s, 0, 0] = block(jnp.where(r < 2, ask1[z, BESIDE + s], ask3[z, BESIDE + s]))
    for ask, ref in ((ask1, out1), (ask2, out2), (ask3, out3)):
        for s in range(ref.shape[0]):
            ref[s, 0, 0] = block(ask[z, s])


def pack(place, asked, own, sib):
    nh = own.shape[2]
    whole = pl.BlockSpec((2, 8, 1, 1, CH, DH), lambda h, kv: (0, 0, h, kv, 0, 0))

    def out(n):
        return pl.BlockSpec((n, 1, 1, BLK, DH), lambda h, kv: (0, h, kv, 0, 0))

    sizes = (BIG, BESIDE, BASE, BESIDE)
    return pl.pallas_call(
        pack_body,
        grid=(nh, 2),
        in_specs=[smem()] * 4 + [whole, whole],
        out_specs=[out(n) for n in sizes],
        out_shape=[jax.ShapeDtypeStruct((n, nh, 2, BLK, DH), jnp.bfloat16) for n in sizes],
        scratch_shapes=[pltpu.VMEM((PLANE * TOK, DH), jnp.bfloat16)],
        compiler_params=params(),
        name="pack",
    )(place, *asked, own, sib)


def dot_t(a, b):
    return lax.dot_general(a, b, (((1,), (1,)), ((), ())), preferred_element_type=jnp.float32)


def lane_sum(p):
    total = p[:, :DH]
    for at in range(DH, p.shape[1], DH):
        total = total + p[:, at : at + DH]
    return total


def by_lane(op, x):
    total = x[:, :DH]
    for at in range(DH, x.shape[1], DH):
        total = op(total, x[:, at : at + DH])
    return total


def listed_pairs(pairs, qs, m, l, acc, top, scores):
    def rows_of(block):
        return pl.ds(pl.multiple_of(jnp.maximum(block, 0) * BLK, BLK), BLK)

    top[...] = m[...]
    for n, (block, k, _) in enumerate(pairs):
        rows = rows_of(block)
        s = jnp.where(block >= 0, dot_t(qs[rows, :], k()) * SCALE, NONE)
        scores[n] = s
        top[rows, :] = jnp.maximum(top[rows, :], s)
    m_new = jnp.broadcast_to(jnp.max(top[...], axis=1, keepdims=True), (TOK, DH))
    fade = jnp.exp2(m[...] - m_new)
    acc[...] = acc[...] * fade
    l[...] = l[...] * fade
    m[...] = m_new
    for n, (block, _, v) in enumerate(pairs):
        rows = rows_of(block)
        p = jnp.exp2(scores[n] - m[rows, :])
        l[rows, :] += p
        acc[rows, :] += jnp.dot(p.astype(jnp.bfloat16), v(), preferred_element_type=jnp.float32)


QT = 256
NONE = -1e30


def near_body(place_ref, plane_ref, q_ref, own_ref, sib_ref, acc_ref, m_ref, l_ref, qs, kf, vf, top, scores):
    r, c = place_ref[1], place_ref[4]
    qs[...] = q_ref[:, 0].reshape(TOK, DH)
    for b in range(2):
        for ref, core in ((own_ref, c), (sib_ref, 1 - c)):
            start = pl.multiple_of((2 * b + core) * TOK, TOK)
            kf[pl.ds(start, TOK), :] = ref[b, :, 0, 0].reshape(TOK, DH)
            vf[pl.ds(start, TOK), :] = ref[b, :, 0, 1].reshape(TOK, DH)
    acc, m, l = acc_ref.at[0], m_ref.at[0], l_ref.at[0]

    def part(index, size):
        return pl.ds(pl.multiple_of(index * size, size), size)

    third = (r > 0) & (r < PLANE - 1)
    frames = [part(i, TOK) for i in (r, jnp.where(r == 0, 1, r - 1), jnp.where(third, r + 1, r))]

    def tile(t, carry):
        rows = part(t, QT)
        q = qs[rows, :]
        scored = [dot_t(q, kf[at, :]) * SCALE for at in frames]
        scored[2] = jnp.where(third, scored[2], NONE)
        tops = [by_lane(jnp.maximum, s) for s in scored]
        best = jnp.max(jnp.maximum(jnp.maximum(tops[0], tops[1]), tops[2]), axis=1, keepdims=True)
        total = mixed = 0.0
        for s, at in zip(scored, frames, strict=True):
            p = jnp.exp2(s - best)
            total = total + by_lane(jnp.add, p)
            mixed = mixed + jnp.dot(p.astype(jnp.bfloat16), vf[at, :], preferred_element_type=jnp.float32)
        m[rows, :] = jnp.broadcast_to(best, (QT, DH))
        l[rows, :] = total
        acc[rows, :] = mixed
        return carry

    lax.fori_loop(0, TOK // QT, tile, jnp.int32(0))

    def pair(p):
        at = part(plane_ref[2 * p + 1], BLK)
        return plane_ref[2 * p], lambda: kf[at, :], lambda: vf[at, :]

    listed_pairs([pair(p) for p in range(8)], qs, m, l, acc, top, scores)


def head_specs():
    tokens = pl.BlockSpec((8, 1, CH, DH), lambda h: (0, h, 0, 0))
    state = pl.BlockSpec((1, TOK, DH), lambda h: (h, 0, 0))
    return tokens, state


def state_shapes(nh):
    return [jax.ShapeDtypeStruct((nh, TOK, DH), jnp.float32)] * 3


def near(place, plane_pairs, q, own, sib):
    nh = own.shape[2]
    frames = pl.BlockSpec((2, 8, 1, 2, CH, DH), lambda h: (0, 0, h, 0, 0, 0))
    tokens, state = head_specs()
    return pl.pallas_call(
        near_body,
        grid=(nh,),
        in_specs=[smem(), smem(), tokens, frames, frames],
        out_specs=[state] * 3,
        out_shape=state_shapes(nh),
        scratch_shapes=[
            pltpu.VMEM((TOK, DH), jnp.bfloat16),
            pltpu.VMEM((PLANE * TOK, DH), jnp.bfloat16),
            pltpu.VMEM((PLANE * TOK, DH), jnp.bfloat16),
            pltpu.VMEM((TOK, DH), jnp.float32),
            pltpu.VMEM((8, BLK, BLK), jnp.float32),
        ],
        compiler_params=params(),
        name="near",
    )(place, plane_pairs, q, own, sib)


def slots(z, qslot_ref, shift, ref):
    zp = (z + 4 - shift) % 4
    for s in range(ref.shape[0]):
        yield qslot_ref[zp * BESIDE + s], lambda s=s: ref[s, 0, 0], lambda s=s: ref[s, 0, 1]


def beside_body(
    place_ref, qslot_ref, q_ref, big_ref, in1, in3, acc_in, m_in, l_in, acc_ref, m_ref, l_ref, qs, kf, vf, top, scores
):
    z, r = place_ref[0], place_ref[1]
    touches = ((r == 0) & (z > 0)) | ((r == PLANE - 1) & (z < 3))
    qs[...] = q_ref[:, 0].reshape(TOK, DH)

    @pl.when(touches)
    def _():
        for kv, ref in ((0, kf), (1, vf)):
            ref[: BIG * BLK] = big_ref[:, 0, kv].reshape(BIG * BLK, DH)
            for n in range(BIG, NB):
                s = BASE + 1 + n - BIG
                ref[n * BLK : (n + 1) * BLK] = jnp.where(r == 0, in1[s, 0, kv], in3[s, 0, kv])
        for t in range(TOK // QT):
            rows = slice(t * QT, (t + 1) * QT)
            s = dot_t(qs[rows], kf[...]) * SCALE
            m_old = m_in[0, rows]
            m_new = jnp.maximum(m_old, jnp.max(by_lane(jnp.maximum, s), axis=1, keepdims=True))
            p = jnp.exp2(s - m_new[:, :1])
            fade = jnp.exp2(m_old - m_new)
            m_ref[0, rows] = m_new
            l_ref[0, rows] = l_in[0, rows] * fade + by_lane(jnp.add, p)
            mixed = jnp.dot(p.astype(jnp.bfloat16), vf[...], preferred_element_type=jnp.float32)
            acc_ref[0, rows] = acc_in[0, rows] * fade + mixed

    @pl.when(jnp.logical_not(touches))
    def _():
        acc_ref[...] = acc_in[...]
        m_ref[...] = m_in[...]
        l_ref[...] = l_in[...]

    pairs = [*slots(z, qslot_ref, 1, in1), *slots(z, qslot_ref, 3, in3)]
    listed_pairs(pairs, qs, m_ref.at[0], l_ref.at[0], acc_ref.at[0], top, scores)


def block_specs(arrays):
    return [pl.BlockSpec((x.shape[0], 1, 2, BLK, DH), lambda h: (0, h, 0, 0, 0)) for x in arrays]


def beside(place, qslot, q, big, in1, in3, state):
    nh = big.shape[1]
    tokens, held = head_specs()
    return pl.pallas_call(
        beside_body,
        grid=(nh,),
        in_specs=[smem(), smem(), tokens] + block_specs((big, in1, in3)) + [held] * 3,
        out_specs=[held] * 3,
        out_shape=state_shapes(nh),
        scratch_shapes=[pltpu.VMEM((TOK, DH), jnp.bfloat16)] * 3
        + [pltpu.VMEM((TOK, DH), jnp.float32), pltpu.VMEM((2 * BESIDE, BLK, BLK), jnp.float32)],
        compiler_params=params(),
        name="beside",
    )(place, qslot, q, big, in1, in3, *state)


def across_body(place_ref, qslot_ref, q_ref, acc_in, m_in, l_in, in2, o_ref, qs, acc, m, l, top, scores):
    qs[...] = q_ref[:, 0].reshape(TOK, DH)
    acc[...] = acc_in[0]
    m[...] = m_in[0]
    l[...] = l_in[0]
    listed_pairs([*slots(place_ref[0], qslot_ref, 2, in2)], qs, m, l, acc, top, scores)
    total = jnp.sum(l[...], axis=1, keepdims=True)
    o_ref[:, 0] = (acc[...] / total).astype(jnp.bfloat16).reshape(8, CH, DH)


def across(place, qslot, q, state, in2):
    nh = in2.shape[1]
    tokens, held = head_specs()
    return pl.pallas_call(
        across_body,
        grid=(nh,),
        in_specs=[smem(), smem(), tokens, held, held, held] + block_specs((in2,)),
        out_specs=tokens,
        out_shape=jax.ShapeDtypeStruct((8, nh, CH, DH), jnp.bfloat16),
        scratch_shapes=[pltpu.VMEM((TOK, DH), jnp.bfloat16)]
        + [pltpu.VMEM((TOK, DH), jnp.float32)] * 4
        + [pltpu.VMEM((BASE, BLK, BLK), jnp.float32)],
        compiler_params=params(),
        name="across",
    )(place, qslot, q, *state, in2)


def leave_body(groups, *refs):
    *in_refs, o_ref, s = refs
    for ref, rows in zip(in_refs, groups, strict=True):
        for hd in range(8):
            for at, row in enumerate(rows):
                s[pl.ds(hd * PER + row, CH, stride=HEADS), :] = ref[hd, at].astype(jnp.float32)
    o_ref[...] = s[...].reshape(CH, HEADS, DH).astype(jnp.bfloat16)


def leave(parts, groups):
    return pl.pallas_call(
        lambda *refs: leave_body(groups, *refs),
        in_specs=[pl.BlockSpec(memory_space=pltpu.VMEM)] * len(parts),
        out_specs=pl.BlockSpec(memory_space=pltpu.VMEM),
        out_shape=jax.ShapeDtypeStruct((CH, HEADS, DH), jnp.bfloat16),
        scratch_shapes=[pltpu.VMEM((CH * HEADS, DH), jnp.float32)],
        compiler_params=params(),
        name="leave",
    )(*parts)


def at_plane(z, r):
    return PLANE * z + r


TM = ("z", "yh", "c")
BIG_PAIRS = [(at_plane(z, 0), at_plane(z + 1, 0)) for z in range(3)] + [(at_plane(z + 1, 3), at_plane(z, 3)) for z in range(3)]


def together(*values):
    return lax.optimization_barrier(values)


def shards(query, key, value, far_list, far_count):
    z, yh, c, hd = (lax.axis_index(a) for a in ("z", "yh", "c", "head"))
    r = 2 * yh + c
    place = jnp.stack([z, r, PLANE * z + r, hd, c]).astype(i32)
    rates = jnp.asarray(lane_rates())
    def around(x, shift):
        return lax.ppermute(x, "z", [(i, (i + shift) % 4) for i in range(4)])

    def entry(sent):
        nh = sent.shape[2]
        own = lax.all_to_all(sent.reshape(16, nh, 2, CH, DH), ("yh", "head"), 0, 0, tiled=True)
        return own.reshape(2, 8, nh, 2, CH, DH)

    def swap(x):
        return lax.ppermute(x, "c", [(0, 1), (1, 0)])

    def by_head(x):
        return lax.all_to_all(x, "head", 0, 0, tiled=True)

    def send(packed):
        big, *base = packed
        big = lax.ppermute(big, TM, BIG_PAIRS)
        return big, *(around(x, shift) for shift, x in zip((1, 2, 3), base, strict=True))

    sent_a = enter_kv(place, rates, key, value, CHUNKS[0])
    far_list, key, value, sent_a = together(far_list, key, value, sent_a)
    want, qslot, plane_pairs = tables(place, far_list, far_count)
    asked = [around(want, -shift) for shift in (1, 2, 3)]
    sent_b = enter_kv(place, rates, key, value, CHUNKS[1])
    own_a = entry(sent_a)
    own_a, sent_b, asked = together(own_a, sent_b, asked)
    own_b = entry(sent_b)
    sib_a = swap(own_a)
    packed_a = pack(place, asked, own_a, sib_a)
    packed_a, query = together(packed_a, query)
    big_a, in1_a, in2_a, in3_a = send(packed_a)
    q_a, q_b = (enter_q(place, rates, query, rows) for rows in CHUNKS)
    own_b, q_a, q_b, in1_a, in2_a, in3_a = together(own_b, q_a, q_b, in1_a, in2_a, in3_a)
    sib_b = swap(own_b)
    q_a = by_head(q_a)
    packed_b = pack(place, asked, own_b, sib_b)
    packed_b, q_a, big_a = together(packed_b, q_a, big_a)
    big_b, in1_b, in2_b, in3_b = send(packed_b)
    q_b = by_head(q_b)
    state_a = near(place, plane_pairs, q_a, own_a, sib_a)
    state_a = beside(place, qslot, q_a, big_a, in1_a, in3_a, state_a)
    done_a = across(place, qslot, q_a, state_a, in2_a)
    out_a = by_head(done_a)
    q_b, _ = together(q_b, done_a)
    state_b = near(place, plane_pairs, q_b, own_b, sib_b)
    state_b = beside(place, qslot, q_b, big_b, in1_b, in3_b, state_b)
    out_b = by_head(across(place, qslot, q_b, state_b, in2_b))
    return leave((out_a, out_b), CHUNKS)


def solution(mesh):
    split = Mesh(mesh.devices.reshape(4, 2, 2, 8), ("z", "yh", "c", "head"))
    tokens = P(("z", "yh", "c", "head"), None, None)
    blocks = P(TM, None)
    return jax.shard_map(
        shards,
        mesh=split,
        in_specs=(tokens, tokens, tokens, blocks, blocks),
        out_specs=tokens,
        check_vma=False,
    )
```

```python
import jax
import jax.numpy as jnp
import numpy as np
from jax import lax
from jax.experimental import pallas as pl
from jax.experimental.pallas import tpu as pltpu
from jax.sharding import Mesh
from jax.sharding import PartitionSpec as P

FW = 80
TOK = 1280
BLK = 128
CH = 160
NB = 10
DH = 128
RT, RH, RW = 16, 56, 56
HEADS = 24
PER = 3
PLANE = 4
THETA = 256.0
SCALE = float(DH**-0.5 * np.log2(np.e))
CHUNKS = ((0,), (1, 2))

BASE = 8
BESIDE = 12
BIG = 8
VMEM = 58 * 2**20

i32 = jnp.int32


def params():
    return pltpu.CompilerParams(vmem_limit_bytes=VMEM)


def smem():
    return pl.BlockSpec(memory_space=pltpu.SMEM)


def table_body(place_ref, list_ref, count_ref, want_ref, qslot_ref, plane_ref, kb_ref, qb_ref):
    z, r = place_ref[0], place_ref[1]
    f = PLANE * z + r

    def frame_lists(g, carry):
        for j in range(8):
            kb_ref[g * 8 + j] = 0
            qb_ref[g * 8 + j] = 0

        def one_block(n, filled):
            kb_ref[g * 8 + filled] = list_ref[n, g] - NB * g
            qb_ref[g * 8 + filled] = n
            return filled + jnp.where(count_ref[n, g] > 0, 1, 0).astype(i32)

        lax.fori_loop(0, NB, one_block, jnp.int32(0))
        return carry

    lax.fori_loop(0, PLANE * 4, frame_lists, jnp.int32(0))

    def clear(s, carry):
        for zp in range(4):
            want_ref[zp, s] = 0
        return carry

    lax.fori_loop(0, 128, clear, jnp.int32(0))
    for s in range(64):
        qslot_ref[s] = -1
    for zp in range(4):
        for i in range(PLANE):
            g = PLANE * zp + i
            far = jnp.abs(f - g) >= 2
            for j in range(2):
                want_ref[zp, 2 * i + j] = NB * i + kb_ref[g * 8 + j]
                qslot_ref[zp * BESIDE + 2 * i + j] = jnp.where(far & (z != zp), qb_ref[g * 8 + j], -1)

    def listed(zp, s, i, j):
        at = (PLANE * zp + i) * 8 + j
        want_ref[zp, s] = NB * i + kb_ref[at]
        qslot_ref[zp * BESIDE + s] = qb_ref[at]

    def side(up, first, second, third):
        zp = z - 1 if up else z + 1
        exists = z > 0 if up else z < 3
        near, two, three = (3, 2, 1) if up else (0, 1, 2)

        @pl.when(exists & (r == first))
        def _():
            for j in range(2):
                listed(zp, 2 * near + j, two, 2 + j)
            listed(zp, BASE, two, 4)
            listed(zp, BESIDE - 1, three, 2)
            for n in range(BIG):
                want_ref[zp, BESIDE + n] = NB * near + n
            for n in range(BIG, NB):
                want_ref[zp, BASE + 1 + n - BIG] = NB * near + n

        @pl.when(exists & (r == second))
        def _():
            listed(zp, BASE, two, 2)
            for j in range(3):
                listed(zp, BASE + 1 + j, near, 2 + j)

        @pl.when(exists & (r == third))
        def _():
            listed(zp, BASE, near, 2)

    side(True, 0, 1, 2)
    side(False, 3, 2, 1)

    two = (r + 2) % PLANE
    three = PLANE - 1 - r
    outer = (r == 0) | (r == PLANE - 1)
    for j in range(5):
        at = (PLANE * z + two) * 8 + j
        plane_ref[2 * j] = qb_ref[at]
        plane_ref[2 * j + 1] = NB * two + kb_ref[at]
    for j in range(3):
        at = (PLANE * z + three) * 8 + j
        plane_ref[10 + 2 * j] = jnp.where(outer, qb_ref[at], -1)
        plane_ref[10 + 2 * j + 1] = NB * three + kb_ref[at]


def tables(place, far_list, far_count):
    return pl.pallas_call(
        table_body,
        in_specs=[smem(), smem(), smem()],
        out_specs=[smem(), smem(), smem()],
        out_shape=[
            jax.ShapeDtypeStruct((4, 128), i32),
            jax.ShapeDtypeStruct((64,), i32),
            jax.ShapeDtypeStruct((16,), i32),
        ],
        scratch_shapes=[pltpu.SMEM((128,), i32), pltpu.SMEM((128,), i32)],
        name="tables",
    )(place, far_list, far_count)


def lane_rates():
    rates = []
    for width in (RT, RH, RW):
        rates.append(np.float32(THETA) ** (np.float32(-2.0) * np.arange(width // 2, dtype=np.float32) / np.float32(width)))
    return np.repeat(np.concatenate(rates), 2)[None].astype(np.float32)


def turn_tables(frame, chunk, rates):
    lane = lax.broadcasted_iota(i32, (CH, DH), 1)
    token = lax.broadcasted_iota(i32, (CH, DH), 0)
    below = (token >= FW).astype(i32)
    position = jnp.where(lane < RT, frame, jnp.where(lane < RT + RH, 2 * chunk + below, token - FW * below))
    angle = position.astype(jnp.float32) * rates
    even = lane % 2 == 0
    sine = jnp.sin(angle)
    return jnp.cos(angle), jnp.where(even, -sine, sine), even


def turn(x, tables_):
    cosine, sine, even = tables_
    swapped = jnp.where(even, pltpu.roll(x, DH - 1, 1), pltpu.roll(x, 1, 1))
    return x * cosine + swapped * sine


def enter_kv_body(rows, place_ref, rates_ref, k_ref, v_ref, o_ref, ks, vs):
    tabs = turn_tables(place_ref[2], place_ref[3], rates_ref[...])
    ks[...] = k_ref[...].astype(jnp.float32).reshape(CH * HEADS, DH)
    vs[...] = v_ref[...].astype(jnp.float32).reshape(CH * HEADS, DH)
    for hd in range(8):
        for at, row in enumerate(rows):
            pick = pl.ds(hd * PER + row, CH, stride=HEADS)
            turned = turn(ks[pick, :], tabs).astype(jnp.bfloat16)
            kept = vs[pick, :].astype(jnp.bfloat16)
            for yh in range(2):
                o_ref[yh, hd, at, 0] = turned
                o_ref[yh, hd, at, 1] = kept


def enter_kv(place, rates, key, value, rows):
    return pl.pallas_call(
        lambda *refs: enter_kv_body(rows, *refs),
        in_specs=[smem()] + [pl.BlockSpec(memory_space=pltpu.VMEM)] * 3,
        out_specs=pl.BlockSpec(memory_space=pltpu.VMEM),
        out_shape=jax.ShapeDtypeStruct((2, 8, len(rows), 2, CH, DH), jnp.bfloat16),
        scratch_shapes=[pltpu.VMEM((CH * HEADS, DH), jnp.float32)] * 2,
        compiler_params=params(),
        name="enter_kv",
    )(place, rates, key, value)


def enter_q_body(rows, place_ref, rates_ref, q_ref, o_ref, qs):
    tabs = turn_tables(place_ref[2], place_ref[3], rates_ref[...])
    qs[...] = q_ref[...].astype(jnp.float32).reshape(CH * HEADS, DH)
    for hd in range(8):
        for at, row in enumerate(rows):
            pick = pl.ds(hd * PER + row, CH, stride=HEADS)
            o_ref[hd, at] = turn(qs[pick, :], tabs).astype(jnp.bfloat16)


def enter_q(place, rates, query, rows):
    return pl.pallas_call(
        lambda *refs: enter_q_body(rows, *refs),
        in_specs=[smem()] + [pl.BlockSpec(memory_space=pltpu.VMEM)] * 2,
        out_specs=pl.BlockSpec(memory_space=pltpu.VMEM),
        out_shape=jax.ShapeDtypeStruct((8, len(rows), CH, DH), jnp.bfloat16),
        scratch_shapes=[pltpu.VMEM((CH * HEADS, DH), jnp.float32)],
        compiler_params=params(),
        name="enter_q",
    )(place, rates, query)


def pack_body(place_ref, ask1, ask2, ask3, own_ref, sib_ref, big_ref, out1, out2, out3, frames):
    z, r, c = place_ref[0], place_ref[1], place_ref[4]
    for b in range(2):
        for ref, core in ((own_ref, c), (sib_ref, 1 - c)):
            start = pl.multiple_of((2 * b + core) * TOK, TOK)
            frames[pl.ds(start, TOK), :] = ref[b, :, 0, 0].reshape(TOK, DH)

    def block(index):
        return frames[pl.ds(pl.multiple_of(index * BLK, BLK), BLK), :]

    for s in range(BIG):
        big_ref[s, 0, 0] = block(jnp.where(r < 2, ask1[z, BESIDE + s], ask3[z, BESIDE + s]))
    for ask, ref in ((ask1, out1), (ask2, out2), (ask3, out3)):
        for s in range(ref.shape[0]):
            ref[s, 0, 0] = block(ask[z, s])


def pack(place, asked, own, sib):
    nh = own.shape[2]
    whole = pl.BlockSpec((2, 8, 1, 1, CH, DH), lambda h, kv: (0, 0, h, kv, 0, 0))

    def out(n):
        return pl.BlockSpec((n, 1, 1, BLK, DH), lambda h, kv: (0, h, kv, 0, 0))

    sizes = (BIG, BESIDE, BASE, BESIDE)
    return pl.pallas_call(
        pack_body,
        grid=(nh, 2),
        in_specs=[smem()] * 4 + [whole, whole],
        out_specs=[out(n) for n in sizes],
        out_shape=[jax.ShapeDtypeStruct((n, nh, 2, BLK, DH), jnp.bfloat16) for n in sizes],
        scratch_shapes=[pltpu.VMEM((PLANE * TOK, DH), jnp.bfloat16)],
        compiler_params=params(),
        name="pack",
    )(place, *asked, own, sib)


def dot_t(a, b):
    return lax.dot_general(a, b, (((1,), (1,)), ((), ())), preferred_element_type=jnp.float32)


def lane_sum(p):
    total = p[:, :DH]
    for at in range(DH, p.shape[1], DH):
        total = total + p[:, at : at + DH]
    return total


def by_lane(op, x):
    total = x[:, :DH]
    for at in range(DH, x.shape[1], DH):
        total = op(total, x[:, at : at + DH])
    return total


def listed_pairs(pairs, qs, m, l, acc, top, scores):
    def rows_of(block):
        return pl.ds(pl.multiple_of(jnp.maximum(block, 0) * BLK, BLK), BLK)

    top[...] = m[...]
    for n, (block, k, _) in enumerate(pairs):
        rows = rows_of(block)
        s = jnp.where(block >= 0, dot_t(qs[rows, :], k()) * SCALE, NONE)
        scores[n] = s
        top[rows, :] = jnp.maximum(top[rows, :], s)
    m_new = jnp.broadcast_to(jnp.max(top[...], axis=1, keepdims=True), (TOK, DH))
    fade = jnp.exp2(m[...] - m_new)
    acc[...] = acc[...] * fade
    l[...] = l[...] * fade
    m[...] = m_new
    for n, (block, _, v) in enumerate(pairs):
        rows = rows_of(block)
        p = jnp.exp2(scores[n] - m[rows, :])
        l[rows, :] += p
        acc[rows, :] += jnp.dot(p.astype(jnp.bfloat16), v(), preferred_element_type=jnp.float32)


QT = 256
NONE = -1e30


def near_body(place_ref, plane_ref, q_ref, own_ref, sib_ref, acc_ref, m_ref, l_ref, qs, kf, vf, top, scores):
    r, c = place_ref[1], place_ref[4]
    qs[...] = q_ref[:, 0].reshape(TOK, DH)
    for b in range(2):
        for ref, core in ((own_ref, c), (sib_ref, 1 - c)):
            start = pl.multiple_of((2 * b + core) * TOK, TOK)
            kf[pl.ds(start, TOK), :] = ref[b, :, 0, 0].reshape(TOK, DH)
            vf[pl.ds(start, TOK), :] = ref[b, :, 0, 1].reshape(TOK, DH)
    acc, m, l = acc_ref.at[0], m_ref.at[0], l_ref.at[0]

    def part(index, size):
        return pl.ds(pl.multiple_of(index * size, size), size)

    def attend(frames):
        def tile(t, carry):
            rows = part(t, QT)
            q = qs[rows, :]
            scored = [dot_t(q, kf[at, :]) * SCALE for at in frames]
            tops = [by_lane(jnp.maximum, s) for s in scored]
            while len(tops) > 1:
                tops = [jnp.maximum(tops[0], tops[1]), *tops[2:]]
            best = jnp.max(tops[0], axis=1, keepdims=True)
            total = mixed = 0.0
            for s, at in zip(scored, frames, strict=True):
                p = jnp.exp2(s - best)
                total = total + by_lane(jnp.add, p)
                mixed = mixed + jnp.dot(p.astype(jnp.bfloat16), vf[at, :], preferred_element_type=jnp.float32)
            m[rows, :] = jnp.broadcast_to(best, (QT, DH))
            l[rows, :] = total
            acc[rows, :] = mixed
            return carry

        lax.fori_loop(0, TOK // QT, tile, jnp.int32(0))

    inner = (r > 0) & (r < PLANE - 1)
    last = PLANE - 1

    @pl.when(inner)
    def _():
        attend([part(i, TOK) for i in (r, jnp.maximum(r - 1, 0), jnp.minimum(r + 1, last))])

    @pl.when(jnp.logical_not(inner))
    def _():
        attend([part(i, TOK) for i in (r, jnp.where(r == 0, 1, last - 1))])

    def pair(p):
        at = part(plane_ref[2 * p + 1], BLK)
        return plane_ref[2 * p], lambda: kf[at, :], lambda: vf[at, :]

    listed_pairs([pair(p) for p in range(8)], qs, m, l, acc, top, scores)


def head_specs():
    tokens = pl.BlockSpec((8, 1, CH, DH), lambda h: (0, h, 0, 0))
    state = pl.BlockSpec((1, TOK, DH), lambda h: (h, 0, 0))
    return tokens, state


def state_shapes(nh):
    return [jax.ShapeDtypeStruct((nh, TOK, DH), jnp.float32)] * 3


def near(place, plane_pairs, q, own, sib):
    nh = own.shape[2]
    frames = pl.BlockSpec((2, 8, 1, 2, CH, DH), lambda h: (0, 0, h, 0, 0, 0))
    tokens, state = head_specs()
    return pl.pallas_call(
        near_body,
        grid=(nh,),
        in_specs=[smem(), smem(), tokens, frames, frames],
        out_specs=[state] * 3,
        out_shape=state_shapes(nh),
        scratch_shapes=[
            pltpu.VMEM((TOK, DH), jnp.bfloat16),
            pltpu.VMEM((PLANE * TOK, DH), jnp.bfloat16),
            pltpu.VMEM((PLANE * TOK, DH), jnp.bfloat16),
            pltpu.VMEM((TOK, DH), jnp.float32),
            pltpu.VMEM((8, BLK, BLK), jnp.float32),
        ],
        compiler_params=params(),
        name="near",
    )(place, plane_pairs, q, own, sib)


def slots(z, qslot_ref, shift, ref):
    zp = (z + 4 - shift) % 4
    for s in range(ref.shape[0]):
        yield qslot_ref[zp * BESIDE + s], lambda s=s: ref[s, 0, 0], lambda s=s: ref[s, 0, 1]


def beside_body(
    place_ref, qslot_ref, q_ref, big_ref, in1, in3, acc_in, m_in, l_in, acc_ref, m_ref, l_ref, qs, kf, vf, top, scores
):
    z, r = place_ref[0], place_ref[1]
    touches = ((r == 0) & (z > 0)) | ((r == PLANE - 1) & (z < 3))
    qs[...] = q_ref[:, 0].reshape(TOK, DH)

    @pl.when(touches)
    def _():
        for kv, ref in ((0, kf), (1, vf)):
            ref[: BIG * BLK] = big_ref[:, 0, kv].reshape(BIG * BLK, DH)
            for n in range(BIG, NB):
                s = BASE + 1 + n - BIG
                ref[n * BLK : (n + 1) * BLK] = jnp.where(r == 0, in1[s, 0, kv], in3[s, 0, kv])
        for t in range(TOK // QT):
            rows = slice(t * QT, (t + 1) * QT)
            s = dot_t(qs[rows], kf[...]) * SCALE
            m_old = m_in[0, rows]
            m_new = jnp.maximum(m_old, jnp.max(by_lane(jnp.maximum, s), axis=1, keepdims=True))
            p = jnp.exp2(s - m_new[:, :1])
            fade = jnp.exp2(m_old - m_new)
            m_ref[0, rows] = m_new
            l_ref[0, rows] = l_in[0, rows] * fade + by_lane(jnp.add, p)
            mixed = jnp.dot(p.astype(jnp.bfloat16), vf[...], preferred_element_type=jnp.float32)
            acc_ref[0, rows] = acc_in[0, rows] * fade + mixed

    @pl.when(jnp.logical_not(touches))
    def _():
        acc_ref[...] = acc_in[...]
        m_ref[...] = m_in[...]
        l_ref[...] = l_in[...]

    pairs = [*slots(z, qslot_ref, 1, in1), *slots(z, qslot_ref, 3, in3)]
    listed_pairs(pairs, qs, m_ref.at[0], l_ref.at[0], acc_ref.at[0], top, scores)


def block_specs(arrays):
    return [pl.BlockSpec((x.shape[0], 1, 2, BLK, DH), lambda h: (0, h, 0, 0, 0)) for x in arrays]


def beside(place, qslot, q, big, in1, in3, state):
    nh = big.shape[1]
    tokens, held = head_specs()
    return pl.pallas_call(
        beside_body,
        grid=(nh,),
        in_specs=[smem(), smem(), tokens] + block_specs((big, in1, in3)) + [held] * 3,
        out_specs=[held] * 3,
        out_shape=state_shapes(nh),
        scratch_shapes=[pltpu.VMEM((TOK, DH), jnp.bfloat16)] * 3
        + [pltpu.VMEM((TOK, DH), jnp.float32), pltpu.VMEM((2 * BESIDE, BLK, BLK), jnp.float32)],
        compiler_params=params(),
        name="beside",
    )(place, qslot, q, big, in1, in3, *state)


def across_body(place_ref, qslot_ref, q_ref, acc_in, m_in, l_in, in2, o_ref, qs, acc, m, l, top, scores):
    qs[...] = q_ref[:, 0].reshape(TOK, DH)
    acc[...] = acc_in[0]
    m[...] = m_in[0]
    l[...] = l_in[0]
    listed_pairs([*slots(place_ref[0], qslot_ref, 2, in2)], qs, m, l, acc, top, scores)
    total = jnp.sum(l[...], axis=1, keepdims=True)
    o_ref[:, 0] = (acc[...] / total).astype(jnp.bfloat16).reshape(8, CH, DH)


def across(place, qslot, q, state, in2):
    nh = in2.shape[1]
    tokens, held = head_specs()
    return pl.pallas_call(
        across_body,
        grid=(nh,),
        in_specs=[smem(), smem(), tokens, held, held, held] + block_specs((in2,)),
        out_specs=tokens,
        out_shape=jax.ShapeDtypeStruct((8, nh, CH, DH), jnp.bfloat16),
        scratch_shapes=[pltpu.VMEM((TOK, DH), jnp.bfloat16)]
        + [pltpu.VMEM((TOK, DH), jnp.float32)] * 4
        + [pltpu.VMEM((BASE, BLK, BLK), jnp.float32)],
        compiler_params=params(),
        name="across",
    )(place, qslot, q, *state, in2)


def leave_body(groups, *refs):
    *in_refs, o_ref, s = refs
    for ref, rows in zip(in_refs, groups, strict=True):
        for hd in range(8):
            for at, row in enumerate(rows):
                s[pl.ds(hd * PER + row, CH, stride=HEADS), :] = ref[hd, at].astype(jnp.float32)
    o_ref[...] = s[...].reshape(CH, HEADS, DH).astype(jnp.bfloat16)


def leave(parts, groups):
    return pl.pallas_call(
        lambda *refs: leave_body(groups, *refs),
        in_specs=[pl.BlockSpec(memory_space=pltpu.VMEM)] * len(parts),
        out_specs=pl.BlockSpec(memory_space=pltpu.VMEM),
        out_shape=jax.ShapeDtypeStruct((CH, HEADS, DH), jnp.bfloat16),
        scratch_shapes=[pltpu.VMEM((CH * HEADS, DH), jnp.float32)],
        compiler_params=params(),
        name="leave",
    )(*parts)


def at_plane(z, r):
    return PLANE * z + r


TM = ("z", "yh", "c")
BIG_PAIRS = [(at_plane(z, 0), at_plane(z + 1, 0)) for z in range(3)] + [(at_plane(z + 1, 3), at_plane(z, 3)) for z in range(3)]


def together(*values):
    return lax.optimization_barrier(values)


def shards(query, key, value, far_list, far_count):
    z, yh, c, hd = (lax.axis_index(a) for a in ("z", "yh", "c", "head"))
    r = 2 * yh + c
    place = jnp.stack([z, r, PLANE * z + r, hd, c]).astype(i32)
    rates = jnp.asarray(lane_rates())
    def around(x, shift):
        return lax.ppermute(x, "z", [(i, (i + shift) % 4) for i in range(4)])

    def entry(sent):
        nh = sent.shape[2]
        own = lax.all_to_all(sent.reshape(16, nh, 2, CH, DH), ("yh", "head"), 0, 0, tiled=True)
        return own.reshape(2, 8, nh, 2, CH, DH)

    def swap(x):
        return lax.ppermute(x, "c", [(0, 1), (1, 0)])

    def by_head(x):
        return lax.all_to_all(x, "head", 0, 0, tiled=True)

    def send(packed):
        big, *base = packed
        big = lax.ppermute(big, TM, BIG_PAIRS)
        return big, *(around(x, shift) for shift, x in zip((1, 2, 3), base, strict=True))

    sent_a = enter_kv(place, rates, key, value, CHUNKS[0])
    far_list, key, value, sent_a = together(far_list, key, value, sent_a)
    want, qslot, plane_pairs = tables(place, far_list, far_count)
    asked = [around(want, -shift) for shift in (1, 2, 3)]
    sent_b = enter_kv(place, rates, key, value, CHUNKS[1])
    own_a = entry(sent_a)
    own_a, sent_b, asked = together(own_a, sent_b, asked)
    own_b = entry(sent_b)
    sib_a = swap(own_a)
    packed_a = pack(place, asked, own_a, sib_a)
    packed_a, query = together(packed_a, query)
    big_a, in1_a, in2_a, in3_a = send(packed_a)
    q_a, q_b = (enter_q(place, rates, query, rows) for rows in CHUNKS)
    own_b, q_a, q_b, in1_a, in2_a, in3_a = together(own_b, q_a, q_b, in1_a, in2_a, in3_a)
    sib_b = swap(own_b)
    q_a = by_head(q_a)
    packed_b = pack(place, asked, own_b, sib_b)
    packed_b, q_a, big_a = together(packed_b, q_a, big_a)
    big_b, in1_b, in2_b, in3_b = send(packed_b)
    q_b = by_head(q_b)
    state_a = near(place, plane_pairs, q_a, own_a, sib_a)
    state_a = beside(place, qslot, q_a, big_a, in1_a, in3_a, state_a)
    done_a = across(place, qslot, q_a, state_a, in2_a)
    out_a = by_head(done_a)
    q_b, _ = together(q_b, done_a)
    state_b = near(place, plane_pairs, q_b, own_b, sib_b)
    state_b = beside(place, qslot, q_b, big_b, in1_b, in3_b, state_b)
    out_b = by_head(across(place, qslot, q_b, state_b, in2_b))
    return leave((out_a, out_b), CHUNKS)


def solution(mesh):
    split = Mesh(mesh.devices.reshape(4, 2, 2, 8), ("z", "yh", "c", "head"))
    tokens = P(("z", "yh", "c", "head"), None, None)
    blocks = P(TM, None)
    return jax.shard_map(
        shards,
        mesh=split,
        in_specs=(tokens, tokens, tokens, blocks, blocks),
        out_specs=tokens,
        check_vma=False,
    )
```

```python
import jax
import jax.numpy as jnp
import numpy as np
from jax import lax
from jax.experimental import pallas as pl
from jax.experimental.pallas import tpu as pltpu
from jax.sharding import Mesh
from jax.sharding import PartitionSpec as P

FW = 80
TOK = 1280
BLK = 128
CH = 160
NB = 10
DH = 128
RT, RH, RW = 16, 56, 56
HEADS = 24
PER = 3
PLANE = 4
THETA = 256.0
SCALE = float(DH**-0.5 * np.log2(np.e))
CHUNKS = ((0,), (1, 2))

BASE = 8
BESIDE = 12
BIG = 8
VMEM = 58 * 2**20

i32 = jnp.int32


def params():
    return pltpu.CompilerParams(vmem_limit_bytes=VMEM)


def smem():
    return pl.BlockSpec(memory_space=pltpu.SMEM)


def table_body(place_ref, list_ref, count_ref, want_ref, qslot_ref, plane_ref, kb_ref, qb_ref):
    z, r = place_ref[0], place_ref[1]
    f = PLANE * z + r

    def frame_lists(g, carry):
        for j in range(8):
            kb_ref[g * 8 + j] = 0
            qb_ref[g * 8 + j] = 0

        def one_block(n, filled):
            kb_ref[g * 8 + filled] = list_ref[n, g] - NB * g
            qb_ref[g * 8 + filled] = n
            return filled + jnp.where(count_ref[n, g] > 0, 1, 0).astype(i32)

        lax.fori_loop(0, NB, one_block, jnp.int32(0))
        return carry

    lax.fori_loop(0, PLANE * 4, frame_lists, jnp.int32(0))

    def clear(s, carry):
        for zp in range(4):
            want_ref[zp, s] = 0
        return carry

    lax.fori_loop(0, 128, clear, jnp.int32(0))
    for s in range(64):
        qslot_ref[s] = -1
    for zp in range(4):
        for i in range(PLANE):
            g = PLANE * zp + i
            far = jnp.abs(f - g) >= 2
            for j in range(2):
                want_ref[zp, 2 * i + j] = NB * i + kb_ref[g * 8 + j]
                qslot_ref[zp * BESIDE + 2 * i + j] = jnp.where(far & (z != zp), qb_ref[g * 8 + j], -1)

    def listed(zp, s, i, j):
        at = (PLANE * zp + i) * 8 + j
        want_ref[zp, s] = NB * i + kb_ref[at]
        qslot_ref[zp * BESIDE + s] = qb_ref[at]

    def side(up, first, second, third):
        zp = z - 1 if up else z + 1
        exists = z > 0 if up else z < 3
        near, two, three = (3, 2, 1) if up else (0, 1, 2)

        @pl.when(exists & (r == first))
        def _():
            for j in range(2):
                listed(zp, 2 * near + j, two, 2 + j)
            listed(zp, BASE, two, 4)
            listed(zp, BESIDE - 1, three, 2)
            for n in range(BIG):
                want_ref[zp, BESIDE + n] = NB * near + n
            for n in range(BIG, NB):
                want_ref[zp, BASE + 1 + n - BIG] = NB * near + n

        @pl.when(exists & (r == second))
        def _():
            listed(zp, BASE, two, 2)
            for j in range(3):
                listed(zp, BASE + 1 + j, near, 2 + j)

        @pl.when(exists & (r == third))
        def _():
            listed(zp, BASE, near, 2)

    side(True, 0, 1, 2)
    side(False, 3, 2, 1)

    two = (r + 2) % PLANE
    three = PLANE - 1 - r
    outer = (r == 0) | (r == PLANE - 1)
    for j in range(5):
        at = (PLANE * z + two) * 8 + j
        plane_ref[2 * j] = qb_ref[at]
        plane_ref[2 * j + 1] = NB * two + kb_ref[at]
    for j in range(3):
        at = (PLANE * z + three) * 8 + j
        plane_ref[10 + 2 * j] = jnp.where(outer, qb_ref[at], -1)
        plane_ref[10 + 2 * j + 1] = NB * three + kb_ref[at]


def tables(place, far_list, far_count):
    return pl.pallas_call(
        table_body,
        in_specs=[smem(), smem(), smem()],
        out_specs=[smem(), smem(), smem()],
        out_shape=[
            jax.ShapeDtypeStruct((4, 128), i32),
            jax.ShapeDtypeStruct((64,), i32),
            jax.ShapeDtypeStruct((16,), i32),
        ],
        scratch_shapes=[pltpu.SMEM((128,), i32), pltpu.SMEM((128,), i32)],
        name="tables",
    )(place, far_list, far_count)


def lane_rates():
    rates = []
    for width in (RT, RH, RW):
        rates.append(np.float32(THETA) ** (np.float32(-2.0) * np.arange(width // 2, dtype=np.float32) / np.float32(width)))
    return np.repeat(np.concatenate(rates), 2)[None].astype(np.float32)


def turn_tables(frame, chunk, rates):
    lane = lax.broadcasted_iota(i32, (CH, DH), 1)
    token = lax.broadcasted_iota(i32, (CH, DH), 0)
    below = (token >= FW).astype(i32)
    position = jnp.where(lane < RT, frame, jnp.where(lane < RT + RH, 2 * chunk + below, token - FW * below))
    angle = position.astype(jnp.float32) * rates
    even = lane % 2 == 0
    sine = jnp.sin(angle)
    return jnp.cos(angle), jnp.where(even, -sine, sine), even


def turn(x, tables_):
    cosine, sine, even = tables_
    swapped = jnp.where(even, pltpu.roll(x, DH - 1, 1), pltpu.roll(x, 1, 1))
    return x * cosine + swapped * sine


def enter_kv_body(rows, place_ref, rates_ref, k_ref, v_ref, o_ref, ks, vs):
    tabs = turn_tables(place_ref[2], place_ref[3], rates_ref[...])
    ks[...] = k_ref[...].astype(jnp.float32).reshape(CH * HEADS, DH)
    vs[...] = v_ref[...].astype(jnp.float32).reshape(CH * HEADS, DH)
    for hd in range(8):
        for at, row in enumerate(rows):
            pick = pl.ds(hd * PER + row, CH, stride=HEADS)
            turned = turn(ks[pick, :], tabs).astype(jnp.bfloat16)
            kept = vs[pick, :].astype(jnp.bfloat16)
            for yh in range(2):
                o_ref[yh, hd, at, 0] = turned
                o_ref[yh, hd, at, 1] = kept


def enter_kv(place, rates, key, value, rows):
    return pl.pallas_call(
        lambda *refs: enter_kv_body(rows, *refs),
        in_specs=[smem()] + [pl.BlockSpec(memory_space=pltpu.VMEM)] * 3,
        out_specs=pl.BlockSpec(memory_space=pltpu.VMEM),
        out_shape=jax.ShapeDtypeStruct((2, 8, len(rows), 2, CH, DH), jnp.bfloat16),
        scratch_shapes=[pltpu.VMEM((CH * HEADS, DH), jnp.float32)] * 2,
        compiler_params=params(),
        name="enter_kv",
    )(place, rates, key, value)


def enter_q_body(rows, place_ref, rates_ref, q_ref, o_ref, qs):
    tabs = turn_tables(place_ref[2], place_ref[3], rates_ref[...])
    qs[...] = q_ref[...].astype(jnp.float32).reshape(CH * HEADS, DH)
    for hd in range(8):
        for at, row in enumerate(rows):
            pick = pl.ds(hd * PER + row, CH, stride=HEADS)
            o_ref[hd, at] = turn(qs[pick, :], tabs).astype(jnp.bfloat16)


def enter_q(place, rates, query, rows):
    return pl.pallas_call(
        lambda *refs: enter_q_body(rows, *refs),
        in_specs=[smem()] + [pl.BlockSpec(memory_space=pltpu.VMEM)] * 2,
        out_specs=pl.BlockSpec(memory_space=pltpu.VMEM),
        out_shape=jax.ShapeDtypeStruct((8, len(rows), CH, DH), jnp.bfloat16),
        scratch_shapes=[pltpu.VMEM((CH * HEADS, DH), jnp.float32)],
        compiler_params=params(),
        name="enter_q",
    )(place, rates, query)


def pack_body(place_ref, ask1, ask2, ask3, own_ref, sib_ref, big_ref, out1, out2, out3, frames):
    z, r, c = place_ref[0], place_ref[1], place_ref[4]
    for b in range(2):
        for ref, core in ((own_ref, c), (sib_ref, 1 - c)):
            start = pl.multiple_of((2 * b + core) * TOK, TOK)
            frames[pl.ds(start, TOK), :] = ref[b, :, 0, 0].reshape(TOK, DH)

    def block(index):
        return frames[pl.ds(pl.multiple_of(index * BLK, BLK), BLK), :]

    for s in range(BIG):
        big_ref[s, 0, 0] = block(jnp.where(r < 2, ask1[z, BESIDE + s], ask3[z, BESIDE + s]))
    for ask, ref in ((ask1, out1), (ask2, out2), (ask3, out3)):
        for s in range(ref.shape[0]):
            ref[s, 0, 0] = block(ask[z, s])


def pack(place, asked, own, sib):
    nh = own.shape[2]
    whole = pl.BlockSpec((2, 8, 1, 1, CH, DH), lambda h, kv: (0, 0, h, kv, 0, 0))

    def out(n):
        return pl.BlockSpec((n, 1, 1, BLK, DH), lambda h, kv: (0, h, kv, 0, 0))

    sizes = (BIG, BESIDE, BASE, BESIDE)
    return pl.pallas_call(
        pack_body,
        grid=(nh, 2),
        in_specs=[smem()] * 4 + [whole, whole],
        out_specs=[out(n) for n in sizes],
        out_shape=[jax.ShapeDtypeStruct((n, nh, 2, BLK, DH), jnp.bfloat16) for n in sizes],
        scratch_shapes=[pltpu.VMEM((PLANE * TOK, DH), jnp.bfloat16)],
        compiler_params=params(),
        name="pack",
    )(place, *asked, own, sib)


def dot_t(a, b):
    return lax.dot_general(a, b, (((1,), (1,)), ((), ())), preferred_element_type=jnp.float32)


def lane_sum(p):
    total = p[:, :DH]
    for at in range(DH, p.shape[1], DH):
        total = total + p[:, at : at + DH]
    return total


def by_lane(op, x):
    total = x[:, :DH]
    for at in range(DH, x.shape[1], DH):
        total = op(total, x[:, at : at + DH])
    return total


def listed_pairs(pairs, qs, m, l, acc, top, scores):
    def rows_of(block):
        return pl.ds(pl.multiple_of(jnp.maximum(block, 0) * BLK, BLK), BLK)

    top[...] = m[...]
    for n, (block, k, _) in enumerate(pairs):
        rows = rows_of(block)
        s = jnp.where(block >= 0, dot_t(qs[rows, :], k()) * SCALE, NONE)
        scores[n] = s
        top[rows, :] = jnp.maximum(top[rows, :], s)
    m_new = jnp.broadcast_to(jnp.max(top[...], axis=1, keepdims=True), (TOK, DH))
    fade = jnp.exp2(m[...] - m_new)
    acc[...] = acc[...] * fade
    l[...] = l[...] * fade
    m[...] = m_new
    for n, (block, _, v) in enumerate(pairs):
        rows = rows_of(block)
        p = jnp.exp2(scores[n] - m[rows, :])
        l[rows, :] += p
        acc[rows, :] += jnp.dot(p.astype(jnp.bfloat16), v(), preferred_element_type=jnp.float32)


QT = 256
NONE = -1e30


def near_body(place_ref, plane_ref, q_ref, own_ref, sib_ref, acc_ref, m_ref, l_ref, qs, kf, vf, top, scores):
    r, c = place_ref[1], place_ref[4]
    qs[...] = q_ref[:, 0].reshape(TOK, DH)
    for b in range(2):
        for ref, core in ((own_ref, c), (sib_ref, 1 - c)):
            start = pl.multiple_of((2 * b + core) * TOK, TOK)
            kf[pl.ds(start, TOK), :] = ref[b, :, 0, 0].reshape(TOK, DH)
            vf[pl.ds(start, TOK), :] = ref[b, :, 0, 1].reshape(TOK, DH)
    acc, m, l = acc_ref.at[0], m_ref.at[0], l_ref.at[0]

    def part(index, size):
        return pl.ds(pl.multiple_of(index * size, size), size)

    def attend(frames):
        def tile(t, carry):
            rows = part(t, QT)
            q = qs[rows, :]
            scored = [dot_t(q, kf[at, :]) * SCALE for at in frames]
            tops = [by_lane(jnp.maximum, s) for s in scored]
            while len(tops) > 1:
                tops = [jnp.maximum(tops[0], tops[1]), *tops[2:]]
            best = jnp.max(tops[0], axis=1, keepdims=True)
            total = mixed = 0.0
            for s, at in zip(scored, frames, strict=True):
                p = jnp.exp2(s - best)
                total = total + by_lane(jnp.add, p)
                mixed = mixed + jnp.dot(p.astype(jnp.bfloat16), vf[at, :], preferred_element_type=jnp.float32)
            m[rows, :] = jnp.broadcast_to(best, (QT, DH))
            l[rows, :] = total
            acc[rows, :] = mixed
            return carry

        lax.fori_loop(0, TOK // QT, tile, jnp.int32(0))

    inner = (r > 0) & (r < PLANE - 1)
    last = PLANE - 1

    @pl.when(inner)
    def _():
        attend([part(i, TOK) for i in (r, jnp.maximum(r - 1, 0), jnp.minimum(r + 1, last))])

    @pl.when(jnp.logical_not(inner))
    def _():
        attend([part(i, TOK) for i in (r, jnp.where(r == 0, 1, last - 1))])

    def pair(p):
        at = part(plane_ref[2 * p + 1], BLK)
        return plane_ref[2 * p], lambda: kf[at, :], lambda: vf[at, :]

    listed_pairs([pair(p) for p in range(8)], qs, m, l, acc, top, scores)


def head_specs():
    tokens = pl.BlockSpec((8, 1, CH, DH), lambda h: (0, h, 0, 0))
    state = pl.BlockSpec((1, TOK, DH), lambda h: (h, 0, 0))
    return tokens, state


def state_shapes(nh):
    return [jax.ShapeDtypeStruct((nh, TOK, DH), jnp.float32)] * 3


def near(place, plane_pairs, q, own, sib):
    nh = own.shape[2]
    frames = pl.BlockSpec((2, 8, 1, 2, CH, DH), lambda h: (0, 0, h, 0, 0, 0))
    tokens, state = head_specs()
    return pl.pallas_call(
        near_body,
        grid=(nh,),
        in_specs=[smem(), smem(), tokens, frames, frames],
        out_specs=[state] * 3,
        out_shape=state_shapes(nh),
        scratch_shapes=[
            pltpu.VMEM((TOK, DH), jnp.bfloat16),
            pltpu.VMEM((PLANE * TOK, DH), jnp.bfloat16),
            pltpu.VMEM((PLANE * TOK, DH), jnp.bfloat16),
            pltpu.VMEM((TOK, DH), jnp.float32),
            pltpu.VMEM((8, BLK, BLK), jnp.float32),
        ],
        compiler_params=params(),
        name="near",
    )(place, plane_pairs, q, own, sib)


def slots(z, qslot_ref, shift, ref):
    zp = (z + 4 - shift) % 4
    for s in range(ref.shape[0]):
        yield qslot_ref[zp * BESIDE + s], lambda s=s: ref[s, 0, 0], lambda s=s: ref[s, 0, 1]


def received(place_ref, qslot_ref, q_ref, big_ref, came, acc_in, m_in, l_in, acc, m, l, qs, kf, vf, top, scores):
    in1, in3 = came[1], came[3]
    z, r = place_ref[0], place_ref[1]
    touches = ((r == 0) & (z > 0)) | ((r == PLANE - 1) & (z < 3))
    qs[...] = q_ref[:, 0].reshape(TOK, DH)

    @pl.when(touches)
    def _():
        for kv, ref in ((0, kf), (1, vf)):
            ref[: BIG * BLK] = big_ref[:, 0, kv].reshape(BIG * BLK, DH)
            for n in range(BIG, NB):
                s = BASE + 1 + n - BIG
                ref[n * BLK : (n + 1) * BLK] = jnp.where(r == 0, in1[s, 0, kv], in3[s, 0, kv])
        for t in range(TOK // QT):
            rows = slice(t * QT, (t + 1) * QT)
            s = dot_t(qs[rows], kf[...]) * SCALE
            m_old = m_in[0, rows]
            m_new = jnp.maximum(m_old, jnp.max(by_lane(jnp.maximum, s), axis=1, keepdims=True))
            p = jnp.exp2(s - m_new[:, :1])
            fade = jnp.exp2(m_old - m_new)
            m[rows] = m_new
            l[rows] = l_in[0, rows] * fade + by_lane(jnp.add, p)
            mixed = jnp.dot(p.astype(jnp.bfloat16), vf[...], preferred_element_type=jnp.float32)
            acc[rows] = acc_in[0, rows] * fade + mixed

    @pl.when(jnp.logical_not(touches))
    def _():
        acc[...] = acc_in[0]
        m[...] = m_in[0]
        l[...] = l_in[0]

    pairs = [pair for shift, ref in came.items() for pair in slots(z, qslot_ref, shift, ref)]
    listed_pairs(pairs, qs, m, l, acc, top, scores)


def beside_body(place_ref, qslot_ref, q_ref, big_ref, in1, in3, acc_in, m_in, l_in, acc_ref, m_ref, l_ref, *scratch):
    state = (acc_ref.at[0], m_ref.at[0], l_ref.at[0])
    received(place_ref, qslot_ref, q_ref, big_ref, {1: in1, 3: in3}, acc_in, m_in, l_in, *state, *scratch)


def all_body(place_ref, qslot_ref, q_ref, big_ref, in1, in2, in3, acc_in, m_in, l_in, o_ref, acc, m, l, *scratch):
    came = {1: in1, 2: in2, 3: in3}
    received(place_ref, qslot_ref, q_ref, big_ref, came, acc_in, m_in, l_in, acc, m, l, *scratch)
    divide(o_ref, acc, l)


def divide(o_ref, acc, l):
    total = jnp.sum(l[...], axis=1, keepdims=True)
    o_ref[:, 0] = (acc[...] / total).astype(jnp.bfloat16).reshape(8, CH, DH)


def block_specs(arrays):
    return [pl.BlockSpec((x.shape[0], 1, 2, BLK, DH), lambda h: (0, h, 0, 0, 0)) for x in arrays]


def beside(place, qslot, q, big, in1, in3, state):
    nh = big.shape[1]
    tokens, held = head_specs()
    return pl.pallas_call(
        beside_body,
        grid=(nh,),
        in_specs=[smem(), smem(), tokens] + block_specs((big, in1, in3)) + [held] * 3,
        out_specs=[held] * 3,
        out_shape=state_shapes(nh),
        scratch_shapes=[pltpu.VMEM((TOK, DH), jnp.bfloat16)] * 3
        + [pltpu.VMEM((TOK, DH), jnp.float32), pltpu.VMEM((2 * BESIDE, BLK, BLK), jnp.float32)],
        compiler_params=params(),
        name="beside",
    )(place, qslot, q, big, in1, in3, *state)


def across_body(place_ref, qslot_ref, q_ref, acc_in, m_in, l_in, in2, o_ref, qs, acc, m, l, top, scores):
    qs[...] = q_ref[:, 0].reshape(TOK, DH)
    acc[...] = acc_in[0]
    m[...] = m_in[0]
    l[...] = l_in[0]
    listed_pairs([*slots(place_ref[0], qslot_ref, 2, in2)], qs, m, l, acc, top, scores)
    divide(o_ref, acc, l)


def everything(place, qslot, q, state, big, in1, in2, in3):
    nh = big.shape[1]
    tokens, held = head_specs()
    return pl.pallas_call(
        all_body,
        grid=(nh,),
        in_specs=[smem(), smem(), tokens] + block_specs((big, in1, in2, in3)) + [held] * 3,
        out_specs=tokens,
        out_shape=jax.ShapeDtypeStruct((8, nh, CH, DH), jnp.bfloat16),
        scratch_shapes=[pltpu.VMEM((TOK, DH), jnp.float32)] * 3
        + [pltpu.VMEM((TOK, DH), jnp.bfloat16)] * 3
        + [pltpu.VMEM((TOK, DH), jnp.float32), pltpu.VMEM((2 * BESIDE + BASE, BLK, BLK), jnp.float32)],
        compiler_params=params(),
        name="everything",
    )(place, qslot, q, big, in1, in2, in3, *state)


def across(place, qslot, q, state, in2):
    nh = in2.shape[1]
    tokens, held = head_specs()
    return pl.pallas_call(
        across_body,
        grid=(nh,),
        in_specs=[smem(), smem(), tokens, held, held, held] + block_specs((in2,)),
        out_specs=tokens,
        out_shape=jax.ShapeDtypeStruct((8, nh, CH, DH), jnp.bfloat16),
        scratch_shapes=[pltpu.VMEM((TOK, DH), jnp.bfloat16)]
        + [pltpu.VMEM((TOK, DH), jnp.float32)] * 4
        + [pltpu.VMEM((BASE, BLK, BLK), jnp.float32)],
        compiler_params=params(),
        name="across",
    )(place, qslot, q, *state, in2)


def leave_body(groups, *refs):
    *in_refs, o_ref, s = refs
    for ref, rows in zip(in_refs, groups, strict=True):
        for hd in range(8):
            for at, row in enumerate(rows):
                s[pl.ds(hd * PER + row, CH, stride=HEADS), :] = ref[hd, at].astype(jnp.float32)
    o_ref[...] = s[...].reshape(CH, HEADS, DH).astype(jnp.bfloat16)


def leave(parts, groups):
    return pl.pallas_call(
        lambda *refs: leave_body(groups, *refs),
        in_specs=[pl.BlockSpec(memory_space=pltpu.VMEM)] * len(parts),
        out_specs=pl.BlockSpec(memory_space=pltpu.VMEM),
        out_shape=jax.ShapeDtypeStruct((CH, HEADS, DH), jnp.bfloat16),
        scratch_shapes=[pltpu.VMEM((CH * HEADS, DH), jnp.float32)],
        compiler_params=params(),
        name="leave",
    )(*parts)


def at_plane(z, r):
    return PLANE * z + r


TM = ("z", "yh", "c")
BIG_PAIRS = [(at_plane(z, 0), at_plane(z + 1, 0)) for z in range(3)] + [(at_plane(z + 1, 3), at_plane(z, 3)) for z in range(3)]


def together(*values):
    return lax.optimization_barrier(values)


def shards(query, key, value, far_list, far_count):
    z, yh, c, hd = (lax.axis_index(a) for a in ("z", "yh", "c", "head"))
    r = 2 * yh + c
    place = jnp.stack([z, r, PLANE * z + r, hd, c]).astype(i32)
    rates = jnp.asarray(lane_rates())
    def around(x, shift):
        return lax.ppermute(x, "z", [(i, (i + shift) % 4) for i in range(4)])

    def entry(sent):
        nh = sent.shape[2]
        own = lax.all_to_all(sent.reshape(16, nh, 2, CH, DH), ("yh", "head"), 0, 0, tiled=True)
        return own.reshape(2, 8, nh, 2, CH, DH)

    def swap(x):
        return lax.ppermute(x, "c", [(0, 1), (1, 0)])

    def by_head(x):
        return lax.all_to_all(x, "head", 0, 0, tiled=True)

    def send(packed):
        big, *base = packed
        big = lax.ppermute(big, TM, BIG_PAIRS)
        return big, *(around(x, shift) for shift, x in zip((1, 2, 3), base, strict=True))

    sent_a = enter_kv(place, rates, key, value, CHUNKS[0])
    far_list, key, value, sent_a = together(far_list, key, value, sent_a)
    want, qslot, plane_pairs = tables(place, far_list, far_count)
    asked = [around(want, -shift) for shift in (1, 2, 3)]
    sent_b = enter_kv(place, rates, key, value, CHUNKS[1])
    own_a = entry(sent_a)
    own_a, sent_b, asked = together(own_a, sent_b, asked)
    own_b = entry(sent_b)
    sib_a = swap(own_a)
    packed_a = pack(place, asked, own_a, sib_a)
    packed_a, query = together(packed_a, query)
    big_a, in1_a, in2_a, in3_a = send(packed_a)
    q_a, q_b = (enter_q(place, rates, query, rows) for rows in CHUNKS)
    own_b, q_a, q_b, in1_a, in2_a, in3_a = together(own_b, q_a, q_b, in1_a, in2_a, in3_a)
    sib_b = swap(own_b)
    packed_b = pack(place, asked, own_b, sib_b)
    packed_b, q_a, big_a = together(packed_b, q_a, big_a)
    big_b, in1_b, in2_b, in3_b = send(packed_b)
    q_a = by_head(q_a)
    q_b = by_head(q_b)
    state_a = near(place, plane_pairs, q_a, own_a, sib_a)
    done_a = everything(place, qslot, q_a, state_a, big_a, in1_a, in2_a, in3_a)
    out_a = by_head(done_a)
    q_b, _ = together(q_b, done_a)
    state_b = near(place, plane_pairs, q_b, own_b, sib_b)
    state_b = beside(place, qslot, q_b, big_b, in1_b, in3_b, state_b)
    out_b = by_head(across(place, qslot, q_b, state_b, in2_b))
    return leave((out_a, out_b), CHUNKS)


def solution(mesh):
    split = Mesh(mesh.devices.reshape(4, 2, 2, 8), ("z", "yh", "c", "head"))
    tokens = P(("z", "yh", "c", "head"), None, None)
    blocks = P(TM, None)
    return jax.shard_map(
        shards,
        mesh=split,
        in_specs=(tokens, tokens, tokens, blocks, blocks),
        out_specs=tokens,
        check_vma=False,
    )
```

```python
import jax
import jax.numpy as jnp
import numpy as np
from jax import lax
from jax.experimental import pallas as pl
from jax.experimental.pallas import tpu as pltpu
from jax.sharding import Mesh
from jax.sharding import PartitionSpec as P

FW = 80
TOK = 1280
BLK = 128
CH = 160
NB = 10
DH = 128
RT, RH, RW = 16, 56, 56
HEADS = 24
PER = 3
PLANE = 4
THETA = 256.0
SCALE = float(DH**-0.5 * np.log2(np.e))
CHUNKS = ((0,), (1, 2))

BASE = 8
BESIDE = 12
BIG = 8
VMEM = 58 * 2**20

i32 = jnp.int32


def params():
    return pltpu.CompilerParams(vmem_limit_bytes=VMEM)


def smem():
    return pl.BlockSpec(memory_space=pltpu.SMEM)


def table_body(place_ref, list_ref, count_ref, want_ref, qslot_ref, plane_ref, kb_ref, qb_ref):
    z, r = place_ref[0], place_ref[1]
    f = PLANE * z + r

    def frame_lists(g, carry):
        for j in range(8):
            kb_ref[g * 8 + j] = 0
            qb_ref[g * 8 + j] = 0

        def one_block(n, filled):
            kb_ref[g * 8 + filled] = list_ref[n, g] - NB * g
            qb_ref[g * 8 + filled] = n
            return filled + jnp.where(count_ref[n, g] > 0, 1, 0).astype(i32)

        lax.fori_loop(0, NB, one_block, jnp.int32(0))
        return carry

    lax.fori_loop(0, PLANE * 4, frame_lists, jnp.int32(0))

    def clear(s, carry):
        for zp in range(4):
            want_ref[zp, s] = 0
        return carry

    lax.fori_loop(0, 128, clear, jnp.int32(0))
    for s in range(64):
        qslot_ref[s] = -1
    for zp in range(4):
        for i in range(PLANE):
            g = PLANE * zp + i
            far = jnp.abs(f - g) >= 2
            for j in range(2):
                want_ref[zp, 2 * i + j] = NB * i + kb_ref[g * 8 + j]
                qslot_ref[zp * BESIDE + 2 * i + j] = jnp.where(far & (z != zp), qb_ref[g * 8 + j], -1)

    def listed(zp, s, i, j):
        at = (PLANE * zp + i) * 8 + j
        want_ref[zp, s] = NB * i + kb_ref[at]
        qslot_ref[zp * BESIDE + s] = qb_ref[at]

    def side(up, first, second, third):
        zp = z - 1 if up else z + 1
        exists = z > 0 if up else z < 3
        near, two, three = (3, 2, 1) if up else (0, 1, 2)

        @pl.when(exists & (r == first))
        def _():
            for j in range(2):
                listed(zp, 2 * near + j, two, 2 + j)
            listed(zp, BASE, two, 4)
            listed(zp, BESIDE - 1, three, 2)
            for n in range(BIG):
                want_ref[zp, BESIDE + n] = NB * near + n
            for n in range(BIG, NB):
                want_ref[zp, BASE + 1 + n - BIG] = NB * near + n

        @pl.when(exists & (r == second))
        def _():
            listed(zp, BASE, two, 2)
            for j in range(3):
                listed(zp, BASE + 1 + j, near, 2 + j)

        @pl.when(exists & (r == third))
        def _():
            listed(zp, BASE, near, 2)

    side(True, 0, 1, 2)
    side(False, 3, 2, 1)

    two = (r + 2) % PLANE
    three = PLANE - 1 - r
    outer = (r == 0) | (r == PLANE - 1)
    for j in range(5):
        at = (PLANE * z + two) * 8 + j
        plane_ref[2 * j] = qb_ref[at]
        plane_ref[2 * j + 1] = NB * two + kb_ref[at]
    for j in range(3):
        at = (PLANE * z + three) * 8 + j
        plane_ref[10 + 2 * j] = jnp.where(outer, qb_ref[at], -1)
        plane_ref[10 + 2 * j + 1] = NB * three + kb_ref[at]


def tables(place, far_list, far_count):
    return pl.pallas_call(
        table_body,
        in_specs=[smem(), smem(), smem()],
        out_specs=[smem(), smem(), smem()],
        out_shape=[
            jax.ShapeDtypeStruct((4, 128), i32),
            jax.ShapeDtypeStruct((64,), i32),
            jax.ShapeDtypeStruct((16,), i32),
        ],
        scratch_shapes=[pltpu.SMEM((128,), i32), pltpu.SMEM((128,), i32)],
        name="tables",
    )(place, far_list, far_count)


def lane_rates():
    rates = []
    for width in (RT, RH, RW):
        rates.append(np.float32(THETA) ** (np.float32(-2.0) * np.arange(width // 2, dtype=np.float32) / np.float32(width)))
    return np.repeat(np.concatenate(rates), 2)[None].astype(np.float32)


def turn_tables(frame, chunk, rates):
    lane = lax.broadcasted_iota(i32, (CH, DH), 1)
    token = lax.broadcasted_iota(i32, (CH, DH), 0)
    below = (token >= FW).astype(i32)
    position = jnp.where(lane < RT, frame, jnp.where(lane < RT + RH, 2 * chunk + below, token - FW * below))
    angle = position.astype(jnp.float32) * rates
    even = lane % 2 == 0
    sine = jnp.sin(angle)
    return jnp.cos(angle), jnp.where(even, -sine, sine), even


def turn(x, tables_):
    cosine, sine, even = tables_
    swapped = jnp.where(even, pltpu.roll(x, DH - 1, 1), pltpu.roll(x, 1, 1))
    return x * cosine + swapped * sine


def enter_kv_body(rows, place_ref, rates_ref, k_ref, v_ref, o_ref, ks, vs):
    tabs = turn_tables(place_ref[2], place_ref[3], rates_ref[...])
    ks[...] = k_ref[...].astype(jnp.float32).reshape(CH * HEADS, DH)
    vs[...] = v_ref[...].astype(jnp.float32).reshape(CH * HEADS, DH)
    for hd in range(8):
        for at, row in enumerate(rows):
            pick = pl.ds(hd * PER + row, CH, stride=HEADS)
            turned = turn(ks[pick, :], tabs).astype(jnp.bfloat16)
            kept = vs[pick, :].astype(jnp.bfloat16)
            for yh in range(2):
                o_ref[yh, hd, at, 0] = turned
                o_ref[yh, hd, at, 1] = kept


def enter_kv(place, rates, key, value, rows):
    return pl.pallas_call(
        lambda *refs: enter_kv_body(rows, *refs),
        in_specs=[smem()] + [pl.BlockSpec(memory_space=pltpu.VMEM)] * 3,
        out_specs=pl.BlockSpec(memory_space=pltpu.VMEM),
        out_shape=jax.ShapeDtypeStruct((2, 8, len(rows), 2, CH, DH), jnp.bfloat16),
        scratch_shapes=[pltpu.VMEM((CH * HEADS, DH), jnp.float32)] * 2,
        compiler_params=params(),
        name="enter_kv",
    )(place, rates, key, value)


def enter_q_body(rows, place_ref, rates_ref, q_ref, o_ref, qs):
    tabs = turn_tables(place_ref[2], place_ref[3], rates_ref[...])
    qs[...] = q_ref[...].astype(jnp.float32).reshape(CH * HEADS, DH)
    for hd in range(8):
        for at, row in enumerate(rows):
            pick = pl.ds(hd * PER + row, CH, stride=HEADS)
            o_ref[hd, at] = turn(qs[pick, :], tabs).astype(jnp.bfloat16)


def enter_q(place, rates, query, rows):
    return pl.pallas_call(
        lambda *refs: enter_q_body(rows, *refs),
        in_specs=[smem()] + [pl.BlockSpec(memory_space=pltpu.VMEM)] * 2,
        out_specs=pl.BlockSpec(memory_space=pltpu.VMEM),
        out_shape=jax.ShapeDtypeStruct((8, len(rows), CH, DH), jnp.bfloat16),
        scratch_shapes=[pltpu.VMEM((CH * HEADS, DH), jnp.float32)],
        compiler_params=params(),
        name="enter_q",
    )(place, rates, query)


def pack_body(place_ref, ask1, ask2, ask3, own_ref, sib_ref, big_ref, out1, out2, out3, frames):
    z, r, c = place_ref[0], place_ref[1], place_ref[4]
    for b in range(2):
        for ref, core in ((own_ref, c), (sib_ref, 1 - c)):
            start = pl.multiple_of((2 * b + core) * TOK, TOK)
            frames[pl.ds(start, TOK), :] = ref[b, :, 0, 0].reshape(TOK, DH)

    def block(index):
        return frames[pl.ds(pl.multiple_of(index * BLK, BLK), BLK), :]

    for s in range(BIG):
        big_ref[s, 0, 0] = block(jnp.where(r < 2, ask1[z, BESIDE + s], ask3[z, BESIDE + s]))
    for ask, ref in ((ask1, out1), (ask2, out2), (ask3, out3)):
        for s in range(ref.shape[0]):
            ref[s, 0, 0] = block(ask[z, s])


def pack(place, asked, own, sib):
    nh = own.shape[2]
    whole = pl.BlockSpec((2, 8, 1, 1, CH, DH), lambda h, kv: (0, 0, h, kv, 0, 0))

    def out(n):
        return pl.BlockSpec((n, 1, 1, BLK, DH), lambda h, kv: (0, h, kv, 0, 0))

    sizes = (BIG, BESIDE, BASE, BESIDE)
    return pl.pallas_call(
        pack_body,
        grid=(nh, 2),
        in_specs=[smem()] * 4 + [whole, whole],
        out_specs=[out(n) for n in sizes],
        out_shape=[jax.ShapeDtypeStruct((n, nh, 2, BLK, DH), jnp.bfloat16) for n in sizes],
        scratch_shapes=[pltpu.VMEM((PLANE * TOK, DH), jnp.bfloat16)],
        compiler_params=params(),
        name="pack",
    )(place, *asked, own, sib)


def dot_t(a, b):
    return lax.dot_general(a, b, (((1,), (1,)), ((), ())), preferred_element_type=jnp.float32)


def lane_sum(p):
    total = p[:, :DH]
    for at in range(DH, p.shape[1], DH):
        total = total + p[:, at : at + DH]
    return total


def by_lane(op, x):
    total = x[:, :DH]
    for at in range(DH, x.shape[1], DH):
        total = op(total, x[:, at : at + DH])
    return total


def listed_pairs(pairs, qs, m, l, acc, top, scores):
    def rows_of(block):
        return pl.ds(pl.multiple_of(jnp.maximum(block, 0) * BLK, BLK), BLK)

    top[...] = m[...]
    for n, (block, k, _) in enumerate(pairs):
        rows = rows_of(block)
        s = jnp.where(block >= 0, dot_t(qs[rows, :], k()) * SCALE, NONE)
        scores[n] = s
        top[rows, :] = jnp.maximum(top[rows, :], s)
    m_new = jnp.broadcast_to(jnp.max(top[...], axis=1, keepdims=True), (TOK, DH))
    fade = jnp.exp2(m[...] - m_new)
    acc[...] = acc[...] * fade
    l[...] = l[...] * fade
    m[...] = m_new
    for n, (block, _, v) in enumerate(pairs):
        rows = rows_of(block)
        p = jnp.exp2(scores[n] - m[rows, :])
        l[rows, :] += p
        acc[rows, :] += jnp.dot(p.astype(jnp.bfloat16), v(), preferred_element_type=jnp.float32)


QT = 256
NONE = -1e30


def near_body(place_ref, plane_ref, q_ref, own_ref, sib_ref, acc_ref, m_ref, l_ref, qs, kf, vf, top, scores):
    r, c = place_ref[1], place_ref[4]
    qs[...] = q_ref[:, 0].reshape(TOK, DH)
    for b in range(2):
        for ref, core in ((own_ref, c), (sib_ref, 1 - c)):
            start = pl.multiple_of((2 * b + core) * TOK, TOK)
            kf[pl.ds(start, TOK), :] = ref[b, :, 0, 0].reshape(TOK, DH)
            vf[pl.ds(start, TOK), :] = ref[b, :, 0, 1].reshape(TOK, DH)
    acc, m, l = acc_ref.at[0], m_ref.at[0], l_ref.at[0]

    def part(index, size):
        return pl.ds(pl.multiple_of(index * size, size), size)

    def attend(frames):
        def tile(t, carry):
            rows = part(t, QT)
            q = qs[rows, :]
            scored = [dot_t(q, kf[at, :]) * SCALE for at in frames]
            tops = [by_lane(jnp.maximum, s) for s in scored]
            while len(tops) > 1:
                tops = [jnp.maximum(tops[0], tops[1]), *tops[2:]]
            best = jnp.max(tops[0], axis=1, keepdims=True)
            total = mixed = 0.0
            for s, at in zip(scored, frames, strict=True):
                p = jnp.exp2(s - best)
                total = total + by_lane(jnp.add, p)
                mixed = mixed + jnp.dot(p.astype(jnp.bfloat16), vf[at, :], preferred_element_type=jnp.float32)
            m[rows, :] = jnp.broadcast_to(best, (QT, DH))
            l[rows, :] = total
            acc[rows, :] = mixed
            return carry

        lax.fori_loop(0, TOK // QT, tile, jnp.int32(0))

    inner = (r > 0) & (r < PLANE - 1)
    last = PLANE - 1

    @pl.when(inner)
    def _():
        attend([part(i, TOK) for i in (r, jnp.maximum(r - 1, 0), jnp.minimum(r + 1, last))])

    @pl.when(jnp.logical_not(inner))
    def _():
        attend([part(i, TOK) for i in (r, jnp.where(r == 0, 1, last - 1))])

    def pair(p):
        at = part(plane_ref[2 * p + 1], BLK)
        return plane_ref[2 * p], lambda: kf[at, :], lambda: vf[at, :]

    listed_pairs([pair(p) for p in range(8)], qs, m, l, acc, top, scores)


def head_specs():
    tokens = pl.BlockSpec((8, 1, CH, DH), lambda h: (0, h, 0, 0))
    state = pl.BlockSpec((1, TOK, DH), lambda h: (h, 0, 0))
    return tokens, state


def state_shapes(nh):
    return [jax.ShapeDtypeStruct((nh, TOK, DH), jnp.float32)] * 3


def near(place, plane_pairs, q, own, sib):
    nh = own.shape[2]
    frames = pl.BlockSpec((2, 8, 1, 2, CH, DH), lambda h: (0, 0, h, 0, 0, 0))
    tokens, state = head_specs()
    return pl.pallas_call(
        near_body,
        grid=(nh,),
        in_specs=[smem(), smem(), tokens, frames, frames],
        out_specs=[state] * 3,
        out_shape=state_shapes(nh),
        scratch_shapes=[
            pltpu.VMEM((TOK, DH), jnp.bfloat16),
            pltpu.VMEM((PLANE * TOK, DH), jnp.bfloat16),
            pltpu.VMEM((PLANE * TOK, DH), jnp.bfloat16),
            pltpu.VMEM((TOK, DH), jnp.float32),
            pltpu.VMEM((8, BLK, BLK), jnp.float32),
        ],
        compiler_params=params(),
        name="near",
    )(place, plane_pairs, q, own, sib)


def slots(z, qslot_ref, shift, ref):
    zp = (z + 4 - shift) % 4
    for s in range(ref.shape[0]):
        yield qslot_ref[zp * BESIDE + s], lambda s=s: ref[s, 0, 0], lambda s=s: ref[s, 0, 1]


def received(place_ref, qslot_ref, q_ref, big_ref, came, acc_in, m_in, l_in, acc, m, l, qs, kf, vf, top, scores):
    in1, in3 = came[1], came[3]
    z, r = place_ref[0], place_ref[1]
    touches = ((r == 0) & (z > 0)) | ((r == PLANE - 1) & (z < 3))
    qs[...] = q_ref[:, 0].reshape(TOK, DH)

    @pl.when(touches)
    def _():
        for kv, ref in ((0, kf), (1, vf)):
            ref[: BIG * BLK] = big_ref[:, 0, kv].reshape(BIG * BLK, DH)
            for n in range(BIG, NB):
                s = BASE + 1 + n - BIG
                ref[n * BLK : (n + 1) * BLK] = jnp.where(r == 0, in1[s, 0, kv], in3[s, 0, kv])
        for t in range(TOK // QT):
            rows = slice(t * QT, (t + 1) * QT)
            s = dot_t(qs[rows], kf[...]) * SCALE
            m_old = m_in[0, rows]
            m_new = jnp.maximum(m_old, jnp.max(by_lane(jnp.maximum, s), axis=1, keepdims=True))
            p = jnp.exp2(s - m_new[:, :1])
            fade = jnp.exp2(m_old - m_new)
            m[rows] = m_new
            l[rows] = l_in[0, rows] * fade + by_lane(jnp.add, p)
            mixed = jnp.dot(p.astype(jnp.bfloat16), vf[...], preferred_element_type=jnp.float32)
            acc[rows] = acc_in[0, rows] * fade + mixed

    @pl.when(jnp.logical_not(touches))
    def _():
        acc[...] = acc_in[0]
        m[...] = m_in[0]
        l[...] = l_in[0]

    pairs = [pair for shift, ref in came.items() for pair in slots(z, qslot_ref, shift, ref)]
    listed_pairs(pairs, qs, m, l, acc, top, scores)


def beside_body(place_ref, qslot_ref, q_ref, big_ref, in1, in3, acc_in, m_in, l_in, acc_ref, m_ref, l_ref, *scratch):
    state = (acc_ref.at[0], m_ref.at[0], l_ref.at[0])
    received(place_ref, qslot_ref, q_ref, big_ref, {1: in1, 3: in3}, acc_in, m_in, l_in, *state, *scratch)


def all_body(place_ref, qslot_ref, q_ref, big_ref, in1, in2, in3, acc_in, m_in, l_in, o_ref, acc, m, l, *scratch):
    came = {1: in1, 2: in2, 3: in3}
    received(place_ref, qslot_ref, q_ref, big_ref, came, acc_in, m_in, l_in, acc, m, l, *scratch)
    divide(o_ref, acc, l)


def divide(o_ref, acc, l):
    total = jnp.sum(l[...], axis=1, keepdims=True)
    o_ref[:, 0] = (acc[...] / total).astype(jnp.bfloat16).reshape(8, CH, DH)


def block_specs(arrays):
    return [pl.BlockSpec((x.shape[0], 1, 2, BLK, DH), lambda h: (0, h, 0, 0, 0)) for x in arrays]


def beside(place, qslot, q, big, in1, in3, state):
    nh = big.shape[1]
    tokens, held = head_specs()
    return pl.pallas_call(
        beside_body,
        grid=(nh,),
        in_specs=[smem(), smem(), tokens] + block_specs((big, in1, in3)) + [held] * 3,
        out_specs=[held] * 3,
        out_shape=state_shapes(nh),
        scratch_shapes=[pltpu.VMEM((TOK, DH), jnp.bfloat16)] * 3
        + [pltpu.VMEM((TOK, DH), jnp.float32), pltpu.VMEM((2 * BESIDE, BLK, BLK), jnp.float32)],
        compiler_params=params(),
        name="beside",
    )(place, qslot, q, big, in1, in3, *state)


def across_body(place_ref, qslot_ref, q_ref, acc_in, m_in, l_in, in2, o_ref, qs, acc, m, l, top, scores):
    qs[...] = q_ref[:, 0].reshape(TOK, DH)
    acc[...] = acc_in[0]
    m[...] = m_in[0]
    l[...] = l_in[0]
    listed_pairs([*slots(place_ref[0], qslot_ref, 2, in2)], qs, m, l, acc, top, scores)
    divide(o_ref, acc, l)


def everything(place, qslot, q, state, big, in1, in2, in3):
    nh = big.shape[1]
    tokens, held = head_specs()
    return pl.pallas_call(
        all_body,
        grid=(nh,),
        in_specs=[smem(), smem(), tokens] + block_specs((big, in1, in2, in3)) + [held] * 3,
        out_specs=tokens,
        out_shape=jax.ShapeDtypeStruct((8, nh, CH, DH), jnp.bfloat16),
        scratch_shapes=[pltpu.VMEM((TOK, DH), jnp.float32)] * 3
        + [pltpu.VMEM((TOK, DH), jnp.bfloat16)] * 3
        + [pltpu.VMEM((TOK, DH), jnp.float32), pltpu.VMEM((2 * BESIDE + BASE, BLK, BLK), jnp.float32)],
        compiler_params=params(),
        name="everything",
    )(place, qslot, q, big, in1, in2, in3, *state)


def across(place, qslot, q, state, in2):
    nh = in2.shape[1]
    tokens, held = head_specs()
    return pl.pallas_call(
        across_body,
        grid=(nh,),
        in_specs=[smem(), smem(), tokens, held, held, held] + block_specs((in2,)),
        out_specs=tokens,
        out_shape=jax.ShapeDtypeStruct((8, nh, CH, DH), jnp.bfloat16),
        scratch_shapes=[pltpu.VMEM((TOK, DH), jnp.bfloat16)]
        + [pltpu.VMEM((TOK, DH), jnp.float32)] * 4
        + [pltpu.VMEM((BASE, BLK, BLK), jnp.float32)],
        compiler_params=params(),
        name="across",
    )(place, qslot, q, *state, in2)


def leave_body(groups, *refs):
    *in_refs, o_ref, s = refs
    for ref, rows in zip(in_refs, groups, strict=True):
        for hd in range(8):
            for at, row in enumerate(rows):
                s[pl.ds(hd * PER + row, CH, stride=HEADS), :] = ref[hd, at].astype(jnp.float32)
    o_ref[...] = s[...].reshape(CH, HEADS, DH).astype(jnp.bfloat16)


def leave(parts, groups):
    return pl.pallas_call(
        lambda *refs: leave_body(groups, *refs),
        in_specs=[pl.BlockSpec(memory_space=pltpu.VMEM)] * len(parts),
        out_specs=pl.BlockSpec(memory_space=pltpu.VMEM),
        out_shape=jax.ShapeDtypeStruct((CH, HEADS, DH), jnp.bfloat16),
        scratch_shapes=[pltpu.VMEM((CH * HEADS, DH), jnp.float32)],
        compiler_params=params(),
        name="leave",
    )(*parts)


def at_plane(z, r):
    return PLANE * z + r


TM = ("z", "yh", "c")
BIG_PAIRS = [(at_plane(z, 0), at_plane(z + 1, 0)) for z in range(3)] + [(at_plane(z + 1, 3), at_plane(z, 3)) for z in range(3)]


def together(*values):
    return lax.optimization_barrier(values)


def shards(query, key, value, far_list, far_count):
    z, yh, c, hd = (lax.axis_index(a) for a in ("z", "yh", "c", "head"))
    r = 2 * yh + c
    place = jnp.stack([z, r, PLANE * z + r, hd, c]).astype(i32)
    rates = jnp.asarray(lane_rates())
    def around(x, shift):
        return lax.ppermute(x, "z", [(i, (i + shift) % 4) for i in range(4)])

    def entry(sent):
        nh = sent.shape[2]
        own = lax.all_to_all(sent.reshape(16, nh, 2, CH, DH), ("yh", "head"), 0, 0, tiled=True)
        return own.reshape(2, 8, nh, 2, CH, DH)

    def swap(x):
        return lax.ppermute(x, "c", [(0, 1), (1, 0)])

    def by_head(x):
        return lax.all_to_all(x, "head", 0, 0, tiled=True)

    def send(packed):
        big, *base = packed
        big = lax.ppermute(big, TM, BIG_PAIRS)
        return big, *(around(x, shift) for shift, x in zip((1, 2, 3), base, strict=True))

    sent_a = enter_kv(place, rates, key, value, CHUNKS[0])
    far_list, key, value, sent_a = together(far_list, key, value, sent_a)
    want, qslot, plane_pairs = tables(place, far_list, far_count)
    asked = [around(want, -shift) for shift in (1, 2, 3)]
    sent_b = enter_kv(place, rates, key, value, CHUNKS[1])
    own_a = entry(sent_a)
    own_a, sent_b, asked = together(own_a, sent_b, asked)
    own_b = entry(sent_b)
    sib_a = swap(own_a)
    packed_a = pack(place, asked, own_a, sib_a)
    packed_a, query = together(packed_a, query)
    big_a, in1_a, in2_a, in3_a = send(packed_a)
    q_a, q_b = (enter_q(place, rates, query, rows) for rows in CHUNKS)
    own_b, q_a, q_b, big_a, in1_a, in3_a = together(own_b, q_a, q_b, big_a, in1_a, in3_a)
    sib_b = swap(own_b)
    packed_b = pack(place, asked, own_b, sib_b)
    packed_b, q_a, in2_a = together(packed_b, q_a, in2_a)
    big_b, in1_b, in2_b, in3_b = send(packed_b)
    q_a = by_head(q_a)
    q_b = by_head(q_b)
    state_a = near(place, plane_pairs, q_a, own_a, sib_a)
    done_a = everything(place, qslot, q_a, state_a, big_a, in1_a, in2_a, in3_a)
    out_a = by_head(done_a)
    q_b, _ = together(q_b, done_a)
    state_b = near(place, plane_pairs, q_b, own_b, sib_b)
    state_b = beside(place, qslot, q_b, big_b, in1_b, in3_b, state_b)
    out_b = by_head(across(place, qslot, q_b, state_b, in2_b))
    return leave((out_a, out_b), CHUNKS)


def solution(mesh):
    split = Mesh(mesh.devices.reshape(4, 2, 2, 8), ("z", "yh", "c", "head"))
    tokens = P(("z", "yh", "c", "head"), None, None)
    blocks = P(TM, None)
    return jax.shard_map(
        shards,
        mesh=split,
        in_specs=(tokens, tokens, tokens, blocks, blocks),
        out_specs=tokens,
        check_vma=False,
    )
```
